512 devices in a mesh: lon: 32 (over z_hi, y, core), lat: 16 (over z_lo, x).
Axes of the slice: x: 4, y: 8, z: 8 (z_hi: 2, z_lo: 4; z = z_hi * 4 + z_lo), core: 2. Of those that a mesh axis runs over, the one named last changes fastest.
Arguments:
- tracer: float32 [8, 2048, 8192], P(None, 'lat', 'lon'), may hold values from -8 to 8
- courant: float32 [8, 2048, 8192], P(None, 'lat', 'lon'), may hold values from 0.25 to 40960
- hop_counts: int32 [2048], P('lat'), may hold values from 0 to 7, as said below
- row_area: float32 [2048], P('lat'), may hold values from 1 to 10
Outputs:
- updated: float32 [8, 2048, 8192], P(None, 'lat', 'lon')
- dateline_flux: float32 [8], replicated
The draws below stay inside these ranges and needn't reach their ends.
Inputs may be any that keep to these rules, and one draw needn't show every extreme that they name: `hop_counts`: only the first 8 and the last 8 latitude rows may have counts above 0.
All inputs are finite; a program needn't handle non-finite values.
Results may differ from the reference program's by a relative error of at most 0.0003.
Values sent between devices are 32-bit elements; how exact they have to be, the bound alone decides.
No kernel may reach another device: no remote copies, remote signals or barrier semaphores. Data moves between devices by JAX's collectives and lax.ppermute only.
A program may use at most 64 MiB of HBM per device.

```python
import math
import jax
import jax.numpy as jnp
from jax import lax

CELLS = 256
VERTICAL_LAYERS = 8
POLAR = 8
STOPS = 7
LONGITUDE_COUNT = 8192
LATITUDE_ROWS = 2048


def draw_tracer(key, part):
    first = jax.random.fold_in(key, 0)
    values = jax.random.normal(first, (VERTICAL_LAYERS, LATITUDE_ROWS, LONGITUDE_COUNT), jnp.float32)
    return jnp.clip(values, -8.0, 8.0)


def draw_courant(key, part):
    random_keys = jax.random.split(key, 7)
    starting_point = jnp.exp(jax.random.uniform(random_keys[1], (VERTICAL_LAYERS, LATITUDE_ROWS, 1), jnp.float32, jnp.log(0.5), jnp.log(5.0)))
    rows = jnp.arange(LATITUDE_ROWS, dtype=jnp.float32)
    latitude = (rows + 0.5) / LATITUDE_ROWS * jnp.pi - 0.5 * jnp.pi
    broaden_range = 1.0 / jnp.cos(latitude)
    coarse_estimate = jax.random.uniform(random_keys[3], (VERTICAL_LAYERS, LATITUDE_ROWS, LONGITUDE_COUNT), jnp.float32, 0.5, 1.5)
    row_index = jnp.arange(LATITUDE_ROWS, dtype=jnp.int32)
    polar_rows = (row_index < POLAR) | (row_index >= LATITUDE_ROWS - POLAR)
    polar_factor = jax.random.uniform(random_keys[6], (VERTICAL_LAYERS, LATITUDE_ROWS, 1), jnp.float32, 1.0, 2.0)
    polar_value = LONGITUDE_COUNT * polar_factor * coarse_estimate
    drawn_value = starting_point * coarse_estimate * broaden_range[None, :, None]
    base_value = jnp.where(polar_rows[None, :, None], polar_value, drawn_value)
    cell_positions = jax.random.randint(random_keys[4], (VERTICAL_LAYERS, LATITUDE_ROWS, 2), 0, LONGITUDE_COUNT)
    grid_cells = jnp.arange(LONGITUDE_COUNT, dtype=jnp.int32)[None, None, :]
    sudden_release = (grid_cells == cell_positions[:, :, 0:1]) | (grid_cells == cell_positions[:, :, 1:2])
    release_value = jax.random.uniform(random_keys[5], (VERTICAL_LAYERS, LATITUDE_ROWS, LONGITUDE_COUNT), jnp.float32, 1.0, 4.0)
    return jnp.where(sudden_release, release_value, base_value)


def draw_hop_counts(key, part):
    values = jax.random.randint(key, (LATITUDE_ROWS,), 0, STOPS + 1)
    rows = jnp.arange(LATITUDE_ROWS, dtype=jnp.int32)
    polar = (rows < POLAR) | (rows >= LATITUDE_ROWS - POLAR)
    values = jnp.where(polar, values, 0)
    return jnp.where(rows == 0, STOPS, values).astype(jnp.int32)


def shard_levels(rng, extent, pieces, smallest, high):
    factor_of, own = 1.0, jax.random.fold_in(rng, 6)
    for position, blocks in pieces:
        draws = jnp.exp(jax.random.uniform(jax.random.fold_in(own, position), (blocks,), jnp.float32, smallest / len(pieces), high / len(pieces)))
        factor_of = factor_of * jnp.repeat(draws, extent[position] // blocks).reshape([-1 if axis == position else 1 for axis in range(len(extent))])
    return factor_of


def setup_inputs(seed: int = 0) -> dict:
    splits = jax.random.split(jax.random.key(seed), 5)
    return {
        "tracer": draw_tracer(jax.random.fold_in(splits[4], 71), 0),
        "courant": draw_courant(jax.random.fold_in(splits[4], 71), 0),
        "hop_counts": draw_hop_counts(jax.random.fold_in(splits[4], 71), 0),
        "row_area": jnp.clip(jnp.exp(math.log(10.0) - 2.3025851 * jax.random.uniform(splits[3], (LATITUDE_ROWS,), jnp.float32) ** shard_levels(splits[3], (LATITUDE_ROWS,), ((0, 16),), -0.2, 0.2)), 1.0, 10.0),
    }


def roll_rows(rows, amount):
    return jnp.roll(rows, amount, axis=-1)


def reference(tracer, courant, hop_counts, row_area):
    amounts = (hop_counts * CELLS).astype(jnp.int32)
    shifted = jax.vmap(roll_rows, in_axes=(1, 0), out_axes=1)(tracer, amounts)
    ratios = courant / (1.0 + courant)
    source_t = jnp.moveaxis(shifted, 2, 0)
    ratios_t = jnp.moveaxis(ratios, 2, 0)

    def first_pass(state_pair, inputs):
        source, factor = inputs
        return (state_pair[0] * factor, factor * (source + state_pair[1])), None

    ones = jnp.ones(tracer.shape[:2], jnp.float32)
    zeros = jnp.zeros(tracer.shape[:2], jnp.float32)
    (growth, offset), unused = lax.scan(first_pass, (ones, zeros), (source_t, ratios_t))
    wrap = offset / (1.0 - growth)

    def second_pass(inflow, inputs):
        source, factor = inputs
        return factor * (source + inflow), inflow

    unused_last, before = lax.scan(second_pass, wrap, (source_t, ratios_t))
    updated = (shifted + jnp.moveaxis(before, 0, 2)) / (1.0 + courant)
    dateline_flux = jnp.sum(row_area[None, :] * wrap, axis=1) / jnp.sum(row_area)
    return updated, dateline_flux
```

```python
import jax
import jax.numpy as jnp
from jax import lax
from jax.experimental import pallas as pl
from jax.experimental.pallas import tpu as pltpu
from jax.sharding import Mesh, PartitionSpec as P

HALVES, RING, LEVELS, ROWS, CELLS, SLAB = 2, 16, 8, 128, 256, 8
SEGMENTS = 8
STEPS = CELLS // SEGMENTS
SENT = 40
BACK = 16

VMEM = pl.BlockSpec(memory_space=pltpu.VMEM)
SMEM = pl.BlockSpec(memory_space=pltpu.SMEM)


def lanes(shape):
    return lax.broadcasted_iota(jnp.int32, shape, len(shape) - 1)


def scan_segments(source, courant, put):
    growth = jnp.ones((SEGMENTS, ROWS), jnp.float32)
    offset = jnp.zeros((SEGMENTS, ROWS), jnp.float32)
    for step in range(STEPS):
        at = pl.ds(step, SEGMENTS, stride=STEPS)
        c = courant[at, :]
        inverse = 1.0 / (1.0 + c)
        factor = c * inverse
        total = source[at, :] + offset
        put(at, total * inverse, growth * inverse)
        offset = factor * total
        growth = growth * factor
    place = lax.broadcasted_iota(jnp.int32, (SEGMENTS, ROWS), 0)
    for stride in (1, 2, 4):
        inside = place >= stride
        offset = jnp.where(inside, growth * pltpu.roll(offset, stride, 0) + offset, offset)
        growth = jnp.where(inside, growth * pltpu.roll(growth, stride, 0), growth)
    entry_growth = jnp.where(place >= 1, pltpu.roll(growth, 1, 0), 1.0)
    entry_offset = jnp.where(place >= 1, pltpu.roll(offset, 1, 0), 0.0)
    return entry_growth, entry_offset, growth[-1:], offset[-1:]


def maps_kernel(tracer, courant, maps, part, slope, entry, source_t, courant_t, ends):
    def level(l, slot):
        source_t[slot] = tracer[l].T
        courant_t[slot] = courant[l].T

        def put(at, a, b):
            part[l, at, :] = a
            slope[l, at, :] = b

        g, o, end_g, end_o = scan_segments(source_t.at[slot], courant_t.at[slot], put)
        entry[l, 0] = g
        entry[l, 1] = o
        ends[0, pl.ds(l, 1), :] = end_g
        ends[1, pl.ds(l, 1), :] = end_o

    def pair(i, carry):
        level(2 * i, 0)
        level(2 * i + 1, 1)
        return carry

    lax.fori_loop(0, LEVELS // 2, pair, 0)
    low = lanes((LEVELS, ROWS)) < 64
    g, o = ends[0], ends[1]
    maps[0] = jnp.where(low, g, pltpu.roll(o, 64, 1))
    maps[1] = jnp.where(low, pltpu.roll(g, 64, 1), o)


def local_maps(tracer, courant):
    f32 = jnp.float32
    shape = jax.ShapeDtypeStruct
    return pl.pallas_call(
        maps_kernel,
        out_shape=(
            shape((2, LEVELS, ROWS), f32),
            shape((LEVELS, CELLS, ROWS), f32),
            shape((LEVELS, CELLS, ROWS), f32),
            shape((LEVELS, 2, SEGMENTS, ROWS), f32),
        ),
        in_specs=[VMEM, VMEM],
        out_specs=(VMEM, VMEM, VMEM, VMEM),
        scratch_shapes=[
            pltpu.VMEM((2, CELLS, ROWS), f32),
            pltpu.VMEM((2, CELLS, ROWS), f32),
            pltpu.VMEM((2, LEVELS, ROWS), f32),
        ],
        name="local_maps",
    )(tracer, courant)


def turn_kernel(part, slope, entry, part_out, slope_out, buffer):
    def level(l, slot):
        g, o = entry[l, 0], entry[l, 1]
        for step in range(STEPS):
            at = pl.ds(step, SEGMENTS, stride=STEPS)
            b = slope[l, at, :]
            buffer[slot, 0, at, :] = part[l, at, :] + b * o
            buffer[slot, 1, at, :] = b * g
        part_out[l] = buffer[slot, 0].T
        slope_out[l] = buffer[slot, 1].T

    def pair(i, carry):
        level(2 * i, 0)
        level(2 * i + 1, 1)
        return carry

    lax.fori_loop(0, LEVELS // 2, pair, 0)


def turn(part, slope, entry):
    shape = jax.ShapeDtypeStruct((LEVELS, ROWS, CELLS), jnp.float32)
    return pl.pallas_call(
        turn_kernel,
        out_shape=(shape, shape),
        in_specs=[VMEM, VMEM, VMEM],
        out_specs=(VMEM, VMEM),
        scratch_shapes=[pltpu.VMEM((2, 2, CELLS, ROWS), jnp.float32)],
        name="turn",
    )(part, slope, entry)


def pack_kernel(own, partner, own_maps, partner_maps, sent):
    for r in range(SLAB):
        for a in range(4):
            ref = own if a < 2 else partner
            for half in range(2):
                x = ref[2 * (a % 2) + half, pl.ds(r, LEVELS, stride=SLAB), :]
                to = pl.ds(8 * a + 4 * half, 4)
                sent[2 * r, to, :] = x[:4]
                sent[2 * r + 1, to, :] = x[4:]
    zeros = jnp.zeros((SENT - 32, 128), jnp.float32)
    for l in range(LEVELS):
        for parity in range(2):
            sent[2 * l + parity, pl.ds(32, SENT - 32), :] = zeros
            sent[2 * l + parity, pl.ds(32, 1), :] = own_maps[parity, pl.ds(l, 1), :]
            sent[2 * l + parity, pl.ds(33, 1), :] = partner_maps[parity, pl.ds(l, 1), :]


def pack(own, partner, own_maps, partner_maps):
    return pl.pallas_call(
        pack_kernel,
        out_shape=jax.ShapeDtypeStruct((RING, SENT, 128), jnp.float32),
        in_specs=[VMEM] * 4,
        out_specs=VMEM,
        name="pack",
    )(own, partner, own_maps, partner_maps)


def solve_kernel(scalars, weights, got, back, source, courant, source_t, courant_t, part, slope):
    hop, half, level, parity = scalars[0], scalars[1], scalars[2], scalars[3]
    for d in range(HALVES * RING):
        base = (d % RING) * SENT + (0 if d < RING else 16)
        for side in range(2):
            to = pl.ds(side * 128, 128)
            source[pl.ds(4 * d, 4), to] = got[pl.ds(base + 4 * side, 4), :]
            courant[pl.ds(4 * d, 4), to] = got[pl.ds(base + 8 + 4 * side, 4), :]
    source_t[...] = pltpu.roll(source[...].T, 4 * hop, 1)
    courant_t[...] = courant[...].T

    def put(at, a, b):
        part[at, :] = a
        slope[at, :] = b

    entry_g, entry_o, g, o = scan_segments(source_t, courant_t, put)
    for stride in (4, 8, 16, 32, 64):
        o = g * pltpu.roll(o, stride, 1) + o
        g = g * pltpu.roll(g, stride, 1)
    inflow = pltpu.roll(o / (1.0 - g), 4, 1)
    entry = entry_g * inflow + entry_o
    for step in range(STEPS):
        at = pl.ds(step, SEGMENTS, stride=STEPS)
        source_t[at, :] = part[at, :] + slope[at, :] * entry
    source[...] = source_t[...].T
    x = jnp.concatenate([got[pl.ds(32, RING, stride=SENT), :], got[pl.ds(33, RING, stride=SENT), :]], 0)
    low = lanes(x.shape) < 64
    turned = pltpu.roll(x, 64, 1)
    rest_g = jnp.where(low, x, turned)
    rest_o = jnp.where(low, turned, x)
    for stride in (1, 2, 4, 8, 16):
        rest_o = rest_g * pltpu.roll(rest_o, stride, 0) + rest_o
        rest_g = rest_g * pltpu.roll(rest_g, stride, 0)
    rest = pltpu.roll(rest_o / (1.0 - rest_g), 1, 0)
    wrap = jnp.where(half == 0, rest[:1], rest[RING : RING + 1])
    own = jnp.sum(wrap * weights[pl.ds(0, 1), :], axis=1, keepdims=True)
    lane = lanes((1, 128))
    slab = pltpu.roll(inflow, (4 * parity + 128 - 64 * half) % 128, 1) * weights[pl.ds(1, 1), :]
    means = jnp.where(lane == level, own, 0.0) + jnp.where((lane >= 4 * parity) & (lane < 4 * parity + 4), slab, 0.0)
    zeros = jnp.zeros((BACK - 8, 128), jnp.float32)
    for d in range(RING):
        for side in range(2):
            back[d, pl.ds(4 * side, 4), :] = source[pl.ds(4 * d, 4), pl.ds(side * 128, 128)]
        back[d, pl.ds(8, BACK - 8), :] = zeros
        back[d, pl.ds(8, 1), :] = rest[d : d + 1]
        back[d, pl.ds(9, 1), :] = means


def solve(scalars, weights, got):
    f32 = jnp.float32
    return pl.pallas_call(
        solve_kernel,
        out_shape=jax.ShapeDtypeStruct((RING, BACK, 128), f32),
        in_specs=[SMEM, VMEM, VMEM],
        out_specs=VMEM,
        scratch_shapes=[pltpu.VMEM((ROWS, CELLS), f32)] * 2 + [pltpu.VMEM((CELLS, ROWS), f32)] * 4,
        name="solve",
    )(scalars, weights, got)


def finish_kernel(scalars, part, slope, got, updated):
    low = lanes((LEVELS, ROWS)) < 64
    even = got[pl.ds(8, LEVELS, stride=2 * BACK), :]
    odd = got[pl.ds(8 + BACK, LEVELS, stride=2 * BACK), :]
    inflow = jnp.where(low, even, pltpu.roll(odd, 64, 1))
    columns = jnp.concatenate([inflow] * 16, axis=0).T
    for l in range(LEVELS):
        updated[l] = part[l] + slope[l] * columns[:, l : l + 1]

    @pl.when(scalars[0] == 1)
    def _():
        rows = pl.ds(pl.multiple_of(scalars[1], SLAB), SLAB)
        for l in range(LEVELS):
            for side in range(2):
                at = (l // 4) * BACK + 4 * side + l % 4
                updated[l, rows, pl.ds(side * 128, 128)] = got[pl.ds(at, SLAB, stride=2 * BACK), :]


def finish(scalars, part, slope, got):
    return pl.pallas_call(
        finish_kernel,
        out_shape=jax.ShapeDtypeStruct((LEVELS, ROWS, CELLS), jnp.float32),
        in_specs=[SMEM, VMEM, VMEM, VMEM],
        out_specs=VMEM,
        name="finish",
    )(scalars, part, slope, got)


def body(tracer, courant, hop_counts, row_area):
    lat = lax.axis_index("lat")
    lats = lax.axis_size("lat")
    half = lax.axis_index("half")
    ring = lax.axis_index("ring")
    last = lat == lats - 1
    polar = (lat == 0) | last
    start = jnp.where(last, ROWS - SLAB, 0)

    def slab_of(a):
        a = lax.dynamic_slice_in_dim(a, start, SLAB, 1).reshape(LEVELS * SLAB, CELLS)
        return a[:, :128], a[:, 128:]

    own = jnp.stack([*slab_of(tracer), *slab_of(courant)])

    def across(i):
        h, rest = divmod(i, RING * lats)
        moved = rest % lats in (0, lats - 1)
        return (i, (1 - h) * RING * lats + rest if moved else i)

    every = ("half", "ring", "lat")
    partner = lax.ppermute(own, every, [across(i) for i in range(HALVES * RING * lats)])
    maps, part, slope, entry = local_maps(tracer, courant)
    partner_maps = lax.ppermute(maps, "half", [(0, 1), (1, 0)])
    part, slope = turn(part, slope, entry)

    sent = pack(own, partner, maps, partner_maps)
    got = lax.all_to_all(sent, "ring", 0, 0, tiled=True)

    row = ring // 2
    parity = ring % 2
    position = jnp.arange(ROWS)
    in_slab = polar & (position >= start) & (position < start + SLAB)
    others = jnp.where(in_slab, 0.0, row_area)
    others = jnp.where(parity == 0, others, jnp.roll(others, -64))
    others = jnp.where(position < 64, others, 0.0)
    slab_area = jnp.where(polar, lax.dynamic_index_in_dim(row_area, start + row, 0, False), 0.0)
    weights = jnp.stack([others, jnp.broadcast_to(slab_area, (ROWS,))])
    hop = lax.dynamic_index_in_dim(hop_counts, start + row, 0, False)
    scalars = jnp.stack([hop, half, row, parity]).astype(jnp.int32)
    back = solve(scalars, weights, got.reshape(RING * SENT, 128))
    back = lax.all_to_all(back, "ring", 0, 0, tiled=True)

    sums = jnp.sum(back[:, 9, :], axis=0)
    sums = jnp.where(position == LEVELS, jnp.sum(row_area), sums)
    sums = lax.all_to_all(jnp.broadcast_to(sums, (lats, 1, ROWS)), "lat", 0, 0, tiled=True)
    sums = jnp.sum(sums, axis=(0, 1))
    updated = finish(
        jnp.stack([polar, start]).astype(jnp.int32), part, slope, back.reshape(RING * BACK, 128)
    )
    return updated, sums[:LEVELS] / sums[LEVELS]


def solution(mesh):
    split = Mesh(mesh.devices.reshape(HALVES, RING, -1), ("half", "ring", "lat"))
    field = P(None, "lat", ("half", "ring"))
    return jax.shard_map(
        body,
        mesh=split,
        in_specs=(field, field, P("lat"), P("lat")),
        out_specs=(field, P()),
        check_vma=False,
    )
```

```python
import jax
import jax.numpy as jnp
from jax import lax
from jax.experimental import pallas as pl
from jax.experimental.pallas import tpu as pltpu
from jax.sharding import Mesh, PartitionSpec as P

HALVES, RING, LEVELS, ROWS, CELLS, SLAB = 2, 16, 8, 128, 256, 8
SEGMENTS = 8
STEPS = CELLS // SEGMENTS
SENT = 24
BACK = 16

VMEM = pl.BlockSpec(memory_space=pltpu.VMEM)
SMEM = pl.BlockSpec(memory_space=pltpu.SMEM)


def lanes(shape):
    return lax.broadcasted_iota(jnp.int32, shape, len(shape) - 1)


def scan_segments(source, courant, put):
    growth = jnp.ones((SEGMENTS, ROWS), jnp.float32)
    offset = jnp.zeros((SEGMENTS, ROWS), jnp.float32)
    for step in range(STEPS):
        at = pl.ds(step, SEGMENTS, stride=STEPS)
        c = courant[at, :]
        inverse = 1.0 / (1.0 + c)
        factor = c * inverse
        total = source[at, :] + offset
        put(at, total * inverse, growth * inverse)
        offset = factor * total
        growth = growth * factor
    place = lax.broadcasted_iota(jnp.int32, (SEGMENTS, ROWS), 0)
    for stride in (1, 2, 4):
        inside = place >= stride
        offset = jnp.where(inside, growth * pltpu.roll(offset, stride, 0) + offset, offset)
        growth = jnp.where(inside, growth * pltpu.roll(growth, stride, 0), growth)
    entry_growth = jnp.where(place >= 1, pltpu.roll(growth, 1, 0), 1.0)
    entry_offset = jnp.where(place >= 1, pltpu.roll(offset, 1, 0), 0.0)
    return entry_growth, entry_offset, growth[-1:], offset[-1:]


def scan_kernel(tracer, courant, part, slope, entry, source_t, courant_t):
    def level(l, slot):
        source_t[slot] = tracer[l].T
        courant_t[slot] = courant[l].T

        def put(at, a, b):
            part[l, at, :] = a
            slope[l, at, :] = b

        g, o, _, _ = scan_segments(source_t.at[slot], courant_t.at[slot], put)
        entry[l, 0] = g
        entry[l, 1] = o

    def pair(i, carry):
        level(2 * i, 0)
        level(2 * i + 1, 1)
        return carry

    lax.fori_loop(0, LEVELS // 2, pair, 0)


def scan(tracer, courant):
    f32 = jnp.float32
    shape = jax.ShapeDtypeStruct
    return pl.pallas_call(
        scan_kernel,
        out_shape=(
            shape((LEVELS, CELLS, ROWS), f32),
            shape((LEVELS, CELLS, ROWS), f32),
            shape((LEVELS, 2, SEGMENTS, ROWS), f32),
        ),
        in_specs=[VMEM, VMEM],
        out_specs=(VMEM, VMEM, VMEM),
        scratch_shapes=[pltpu.VMEM((2, CELLS, ROWS), f32)] * 2,
        name="scan",
    )(tracer, courant)


def turn_kernel(part, slope, entry, part_out, slope_out, buffer):
    def level(l, slot):
        g, o = entry[l, 0], entry[l, 1]
        for step in range(STEPS):
            at = pl.ds(step, SEGMENTS, stride=STEPS)
            b = slope[l, at, :]
            buffer[slot, 0, at, :] = part[l, at, :] + b * o
            buffer[slot, 1, at, :] = b * g
        part_out[l] = buffer[slot, 0].T
        slope_out[l] = buffer[slot, 1].T

    def pair(i, carry):
        level(2 * i, 0)
        level(2 * i + 1, 1)
        return carry

    lax.fori_loop(0, LEVELS // 2, pair, 0)


def turn(part, slope, entry):
    shape = jax.ShapeDtypeStruct((LEVELS, ROWS, CELLS), jnp.float32)
    return pl.pallas_call(
        turn_kernel,
        out_shape=(shape, shape),
        in_specs=[VMEM, VMEM, VMEM],
        out_specs=(VMEM, VMEM),
        scratch_shapes=[pltpu.VMEM((2, 2, CELLS, ROWS), jnp.float32)],
        name="turn",
    )(part, slope, entry)


def merge(bit, early, late):
    clear = (lanes((8, 128)) >> bit) % 2 == 0
    step = 1 << bit
    first_g = jnp.where(clear, early[0], pltpu.roll(late[0], step, 1))
    first_o = jnp.where(clear, early[1], pltpu.roll(late[1], step, 1))
    then_g = jnp.where(clear, pltpu.roll(early[0], 128 - step, 1), late[0])
    then_o = jnp.where(clear, pltpu.roll(early[1], 128 - step, 1), late[1])
    return first_g * then_g, then_g * first_o + then_o


def merged(maps, bits):
    for bit in bits:
        maps = [merge(bit, maps[i], maps[i + 1]) for i in range(0, len(maps), 2)]
    return maps[0]


def pack_kernel(tracer, courant, sent, source, factor, slab, sems):
    copies = [
        (
            pltpu.make_async_copy(tracer.at[l], source.at[l], sems.at[0, l]),
            pltpu.make_async_copy(courant.at[l], factor.at[l], sems.at[1, l]),
        )
        for l in range(LEVELS)
    ]
    for pair in copies:
        for copy in pair:
            copy.start()
    last = lax.axis_index("lat") == lax.axis_size("lat") - 1
    start = pl.multiple_of(jnp.where(last, ROWS - SLAB, 0), SLAB)
    sides = ([], [])
    for l in range(LEVELS):
        for copy in copies[l]:
            copy.wait()
        for side in range(2):
            across = pl.ds(128 * side, 128)
            maps = []
            for m in range(ROWS // 8):
                c = factor[l, pl.ds(8 * m, 8), across]
                f = c * (1.0 / (1.0 + c))
                maps.append((f, f * source[l, pl.ds(8 * m, 8), across]))
            sides[side].append(merged(maps, range(4)))
            slab[side, pl.ds(SLAB * l, SLAB), :] = source[l, pl.ds(start, SLAB), across]
            slab[2 + side, pl.ds(SLAB * l, SLAB), :] = factor[l, pl.ds(start, SLAB), across]
    west, east = merged(sides[0], range(4, 7)), merged(sides[1], range(4, 7))
    g, o = west[0] * east[0], east[0] * west[1] + east[1]
    low = lanes((8, 128)) < 64
    rows = (jnp.where(low, g, pltpu.roll(o, 64, 1)), jnp.where(low, pltpu.roll(g, 64, 1), o))
    zeros = jnp.zeros((SENT - 16, 128), jnp.float32)
    for r in range(SLAB):
        for a in range(4):
            x = slab[a, pl.ds(r, LEVELS, stride=SLAB), :]
            sent[2 * r, pl.ds(4 * a, 4), :] = x[:4]
            sent[2 * r + 1, pl.ds(4 * a, 4), :] = x[4:]
        for parity in range(2):
            sent[2 * r + parity, pl.ds(16, SENT - 16), :] = zeros
            sent[2 * r + parity, pl.ds(16, 1), :] = rows[parity][r : r + 1]


def pack(tracer, courant):
    f32 = jnp.float32
    return pl.pallas_call(
        pack_kernel,
        out_shape=pltpu.VMEM((RING, SENT, 128), f32),
        in_specs=[pl.BlockSpec(memory_space=pl.ANY)] * 2,
        out_specs=VMEM,
        scratch_shapes=[
            pltpu.VMEM((LEVELS, ROWS, CELLS), f32),
            pltpu.VMEM((LEVELS, ROWS, CELLS), f32),
            pltpu.VMEM((4, LEVELS * SLAB, 128), f32),
            pltpu.SemaphoreType.DMA((2, LEVELS)),
        ],
        name="pack",
    )(tracer, courant)


def solve_kernel(hops, areas, own, far_slab, far_maps, back, source, courant, source_t, courant_t, part, slope):
    lat = lax.axis_index("lat")
    half = lax.axis_index("half")
    ring = lax.axis_index("ring")
    last = lat == lax.axis_size("lat") - 1
    polar = (lat == 0) | last
    start = jnp.where(last, ROWS - SLAB, 0)
    row, parity = ring // 2, ring % 2
    for d in range(HALVES * RING):
        ref, base = (own, d * SENT) if d < RING else (far_slab, (d - RING) * 16)
        for side in range(2):
            to = pl.ds(side * 128, 128)
            source[pl.ds(4 * d, 4), to] = ref[pl.ds(base + 4 * side, 4), :]
            courant[pl.ds(4 * d, 4), to] = ref[pl.ds(base + 8 + 4 * side, 4), :]
    source_t[...] = pltpu.roll(source[...].T, 4 * hops[start + row], 1)
    courant_t[...] = courant[...].T

    def put(at, a, b):
        part[at, :] = a
        slope[at, :] = b

    entry_g, entry_o, g, o = scan_segments(source_t, courant_t, put)
    for stride in (4, 8, 16, 32, 64):
        o = g * pltpu.roll(o, stride, 1) + o
        g = g * pltpu.roll(g, stride, 1)
    inflow = pltpu.roll(o / (1.0 - g), 4, 1)
    entry = entry_g * inflow + entry_o
    for step in range(STEPS):
        at = pl.ds(step, SEGMENTS, stride=STEPS)
        source_t[at, :] = part[at, :] + slope[at, :] * entry
    source[...] = source_t[...].T
    x = jnp.concatenate([own[pl.ds(16, RING, stride=SENT), :], far_maps[...]], 0)
    low = lanes(x.shape) < 64
    turned = pltpu.roll(x, 64, 1)
    rest_g = jnp.where(low, x, turned)
    rest_o = jnp.where(low, turned, x)
    for stride in (1, 2, 4, 8, 16):
        rest_o = rest_g * pltpu.roll(rest_o, stride, 0) + rest_o
        rest_g = rest_g * pltpu.roll(rest_g, stride, 0)
    rest = pltpu.roll(rest_o / (1.0 - rest_g), 1, 0)
    wrap = jnp.where(half == 0, rest[:1], rest[RING : RING + 1])
    lane = lanes((1, 128))
    from_slab = polar & (lane % 16 == start // SLAB)
    weighted = jnp.where((lane // 64 == parity) & ~from_slab, wrap * areas[pl.ds(row, 1), :], 0.0)
    loops = pltpu.roll(inflow, 64 * ((parity + half) % 2), 1)
    area = jnp.sum(jnp.where(lane == start // SLAB, areas[pl.ds(row, 1), :], 0.0), axis=1, keepdims=True)
    for q in range(4):
        moved = pltpu.roll(loops, 15 * q, 1) if q else loops
        weighted = weighted + jnp.where(polar & (lane == 64 * parity + 16 * q), moved * area, 0.0)
    zeros = jnp.zeros((BACK - 8, 128), jnp.float32)
    for d in range(RING):
        for side in range(2):
            back[d, pl.ds(4 * side, 4), :] = source[pl.ds(4 * d, 4), pl.ds(side * 128, 128)]
        back[d, pl.ds(8, BACK - 8), :] = zeros
        back[d, pl.ds(8, 1), :] = rest[d : d + 1]
        back[d, pl.ds(9, 1), :] = weighted


def solve(hops, areas, own, far_slab, far_maps):
    f32 = jnp.float32
    return pl.pallas_call(
        solve_kernel,
        out_shape=pltpu.VMEM((RING, BACK, 128), f32),
        in_specs=[SMEM] + [VMEM] * 4,
        out_specs=VMEM,
        scratch_shapes=[pltpu.VMEM((ROWS, CELLS), f32)] * 2 + [pltpu.VMEM((CELLS, ROWS), f32)] * 4,
        name="solve",
    )(hops, areas, *[pltpu.with_memory_space_constraint(x, pltpu.VMEM) for x in (own, far_slab, far_maps)])


def spread_kernel(got, area, sums):
    total = jnp.sum(got[pl.ds(9, RING, stride=BACK), :], axis=0, keepdims=True)
    lane = lanes((1, 128))
    total = total + pltpu.roll(total, 120, 1)
    total = jnp.where(lane == 8, jnp.sum(area[...], axis=1, keepdims=True), total)
    for i in range(sums.shape[0]):
        sums[i] = total


def spread(got, area, lats):
    return pl.pallas_call(
        spread_kernel,
        out_shape=jax.ShapeDtypeStruct((lats, 1, 128), jnp.float32),
        in_specs=[VMEM, VMEM],
        out_specs=VMEM,
        name="spread",
    )(pltpu.with_memory_space_constraint(got, pltpu.VMEM), area)


def finish_kernel(part, slope, got, updated):
    low = lanes((8, 128)) < 64
    even = got[pl.ds(8, 8, stride=2 * BACK), :]
    odd = got[pl.ds(8 + BACK, 8, stride=2 * BACK), :]
    inflow = jnp.where(low, even, pltpu.roll(odd, 64, 1))
    for l in range(LEVELS):
        for m in range(ROWS // 8):
            at = pl.ds(8 * m, 8)
            lane = 16 * l + m
            updated[l, at, :] = part[l, at, :] + slope[l, at, :] * inflow[:, lane : lane + 1]
    lat = lax.axis_index("lat")
    last = lat == lax.axis_size("lat") - 1

    @pl.when((lat == 0) | last)
    def _():
        rows = pl.ds(pl.multiple_of(jnp.where(last, ROWS - SLAB, 0), SLAB), SLAB)
        for l in range(LEVELS):
            for side in range(2):
                at = (l // 4) * BACK + 4 * side + l % 4
                updated[l, rows, pl.ds(side * 128, 128)] = got[pl.ds(at, SLAB, stride=2 * BACK), :]


def finish(part, slope, got):
    return pl.pallas_call(
        finish_kernel,
        out_shape=jax.ShapeDtypeStruct((LEVELS, ROWS, CELLS), jnp.float32),
        in_specs=[VMEM, VMEM, VMEM],
        out_specs=VMEM,
        name="finish",
    )(part, slope, pltpu.with_memory_space_constraint(got, pltpu.VMEM))


def mean_kernel(sums, mean):
    total = sums[0]
    for i in range(1, sums.shape[0]):
        total = total + sums[i]
    lane = lanes((1, 128))
    area = jnp.sum(jnp.where(lane == 8, total, 0.0), axis=1, keepdims=True)
    for step in (4, 2, 1):
        total = total + pltpu.roll(total, 128 - step, 1)
    levels = total
    for l in range(1, LEVELS):
        levels = jnp.where(lane == l, pltpu.roll(total, 128 - 15 * l, 1), levels)
    mean[...] = (levels / area)[0, :LEVELS]


def mean(sums):
    return pl.pallas_call(
        mean_kernel,
        out_shape=jax.ShapeDtypeStruct((LEVELS,), jnp.float32),
        in_specs=[VMEM],
        out_specs=VMEM,
        name="mean",
    )(pltpu.with_memory_space_constraint(sums, pltpu.VMEM))


def body(tracer, courant, hop_counts, row_area):
    lats = lax.axis_size("lat")

    def across(i):
        h, rest = divmod(i, RING * lats)
        moved = rest % lats in (0, lats - 1)
        return (i, (1 - h) * RING * lats + rest if moved else i)

    sent = pack(tracer, courant)
    got = lax.all_to_all(sent, "ring", 0, 0, tiled=True)
    every = ("half", "ring", "lat")
    far_slab = lax.ppermute(got[:, :16], every, [across(i) for i in range(HALVES * RING * lats)])
    far_maps = lax.ppermute(got[:, 16], "half", [(0, 1), (1, 0)])
    tracer, courant, got = lax.optimization_barrier((tracer, courant, got))
    scanned = scan(tracer, courant)
    scanned, far_slab = lax.optimization_barrier((scanned, far_slab))
    part, slope = turn(*scanned)
    areas = jnp.tile(row_area.reshape(ROWS // 8, 8).T, (1, 8))
    back = solve(
        hop_counts, areas, got.reshape(RING * SENT, 128), far_slab.reshape(RING * 16, 128), far_maps
    )
    back = lax.all_to_all(back, "ring", 0, 0, tiled=True).reshape(RING * BACK, 128)
    sums = lax.all_to_all(spread(back, row_area.reshape(1, ROWS), lats), "lat", 0, 0, tiled=True)
    return finish(part, slope, back), mean(sums)


def solution(mesh):
    split = Mesh(mesh.devices.reshape(HALVES, RING, -1), ("half", "ring", "lat"))
    field = P(None, "lat", ("half", "ring"))
    return jax.shard_map(
        body,
        mesh=split,
        in_specs=(field, field, P("lat"), P("lat")),
        out_specs=(field, P()),
        check_vma=False,
    )
```

```python
import jax
import jax.numpy as jnp
from jax import lax
from jax.experimental import pallas as pl
from jax.experimental.pallas import tpu as pltpu
from jax.sharding import Mesh, PartitionSpec as P

HALVES, RING, LEVELS, ROWS, CELLS, SLAB = 2, 16, 8, 128, 256, 8
SEGMENTS = 8
STEPS = CELLS // SEGMENTS
SENT = 24
BACK = 16

VMEM = pl.BlockSpec(memory_space=pltpu.VMEM)
SMEM = pl.BlockSpec(memory_space=pltpu.SMEM)


def lanes(shape):
    return lax.broadcasted_iota(jnp.int32, shape, len(shape) - 1)


def polar_start():
    lat = lax.axis_index("lat")
    last = lat == lax.axis_size("lat") - 1
    return (lat == 0) | last, pl.multiple_of(jnp.where(last, ROWS - SLAB, 0), SLAB)


def in_vmem(*arrays):
    return [pltpu.with_memory_space_constraint(x, pltpu.VMEM) for x in arrays]


def pack_kernel(tracer, courant, sent, source_t, courant_t, entries, source, factor, slab, sems):
    copies = [
        (
            pltpu.make_async_copy(tracer.at[l], source.at[l], sems.at[0, l]),
            pltpu.make_async_copy(courant.at[l], factor.at[l], sems.at[1, l]),
        )
        for l in range(LEVELS)
    ]
    for pair in copies:
        for copy in pair:
            copy.start()
    _, start = polar_start()
    for l in range(LEVELS):
        for copy in copies[l]:
            copy.wait()
        source_t[pl.ds(l, CELLS, stride=LEVELS), :] = source[l].T
        courant_t[pl.ds(l, CELLS, stride=LEVELS), :] = factor[l].T
        for side in range(2):
            across = pl.ds(128 * side, 128)
            slab[side, pl.ds(SLAB * l, SLAB), :] = source[l, pl.ds(start, SLAB), across]
            slab[2 + side, pl.ds(SLAB * l, SLAB), :] = factor[l, pl.ds(start, SLAB), across]
    growth = [jnp.ones((LEVELS, ROWS), jnp.float32)] * SEGMENTS
    offset = [jnp.zeros((LEVELS, ROWS), jnp.float32)] * SEGMENTS
    for step in range(STEPS):
        for k in range(SEGMENTS):
            at = pl.ds(LEVELS * (STEPS * k + step), LEVELS)
            c = courant_t[at, :]
            f = c * (1.0 / (1.0 + c))
            offset[k] = f * (source_t[at, :] + offset[k])
            growth[k] = growth[k] * f
    g, o = growth[0], offset[0]
    for k in range(1, SEGMENTS):
        entries[2 * k] = g
        entries[2 * k + 1] = o
        g, o = g * growth[k], growth[k] * o + offset[k]
    low = lanes((LEVELS, ROWS)) < 64
    maps = (jnp.where(low, g, pltpu.roll(o, 64, 1)), jnp.where(low, pltpu.roll(g, 64, 1), o))
    zeros = jnp.zeros((SENT - 16, 128), jnp.float32)
    for r in range(SLAB):
        for a in range(4):
            x = slab[a, pl.ds(r, LEVELS, stride=SLAB), :]
            sent[2 * r, pl.ds(4 * a, 4), :] = x[:4]
            sent[2 * r + 1, pl.ds(4 * a, 4), :] = x[4:]
        for parity in range(2):
            sent[2 * r + parity, pl.ds(16, SENT - 16), :] = zeros
            sent[2 * r + parity, pl.ds(16, 1), :] = maps[parity][r : r + 1]


def pack(tracer, courant):
    f32 = jnp.float32
    return pl.pallas_call(
        pack_kernel,
        out_shape=(
            pltpu.VMEM((RING, SENT, 128), f32),
            pltpu.VMEM((CELLS * LEVELS, ROWS), f32),
            pltpu.VMEM((CELLS * LEVELS, ROWS), f32),
            pltpu.VMEM((2 * SEGMENTS, LEVELS, ROWS), f32),
        ),
        in_specs=[pl.BlockSpec(memory_space=pl.ANY)] * 2,
        out_specs=(VMEM,) * 4,
        scratch_shapes=[
            pltpu.VMEM((LEVELS, ROWS, CELLS), f32),
            pltpu.VMEM((LEVELS, ROWS, CELLS), f32),
            pltpu.VMEM((4, LEVELS * SLAB, 128), f32),
            pltpu.SemaphoreType.DMA((2, LEVELS)),
        ],
        name="pack",
    )(tracer, courant)


def solve_kernel(hops, area, own, far_slab, far_maps, back, source, courant, source_t, courant_t):
    half = lax.axis_index("half")
    ring = lax.axis_index("ring")
    polar, start = polar_start()
    row, parity = ring // 2, ring % 2
    for d in range(HALVES * RING):
        ref, base = (own, d * SENT) if d < RING else (far_slab, (d - RING) * 16)
        for side in range(2):
            to = pl.ds(side * 128, 128)
            source[pl.ds(4 * d, 4), to] = ref[pl.ds(base + 4 * side, 4), :]
            courant[pl.ds(4 * d, 4), to] = ref[pl.ds(base + 8 + 4 * side, 4), :]
    source_t[...] = pltpu.roll(source[...].T, 4 * hops[start + row], 1)
    courant_t[...] = courant[...].T
    parts = range(CELLS // 64)
    growth = [jnp.ones((8, ROWS), jnp.float32) for k in parts]
    offset = [jnp.zeros((8, ROWS), jnp.float32) for k in parts]
    for step in range(8):
        for k in parts:
            at = pl.ds(64 * k + step, 8, stride=8)
            c = courant_t[at, :]
            f = c * (1.0 / (1.0 + c))
            offset[k] = f * (source_t[at, :] + offset[k])
            growth[k] = growth[k] * f
    place = lax.broadcasted_iota(jnp.int32, (8, ROWS), 0)
    for stride in (1, 2, 4):
        inside = place >= stride
        for k in parts:
            offset[k] = jnp.where(inside, growth[k] * pltpu.roll(offset[k], stride, 0) + offset[k], offset[k])
            growth[k] = jnp.where(inside, growth[k] * pltpu.roll(growth[k], stride, 0), growth[k])
    g = jnp.ones((1, ROWS), jnp.float32)
    o = jnp.zeros((1, ROWS), jnp.float32)
    entry = []
    for k in parts:
        first = place == 0
        before_g = jnp.where(first, 1.0, pltpu.roll(growth[k], 1, 0))
        before_o = jnp.where(first, 0.0, pltpu.roll(offset[k], 1, 0))
        entry.append((before_g * g, before_g * o + before_o))
        g, o = g * growth[k][7:], growth[k][7:] * o + offset[k][7:]
    for stride in (4, 8, 16, 32, 64):
        o = g * pltpu.roll(o, stride, 1) + o
        g = g * pltpu.roll(g, stride, 1)
    inflow = pltpu.roll(o / (1.0 - g), 4, 1)
    flux = [entry[k][0] * inflow + entry[k][1] for k in parts]
    for step in range(8):
        for k in parts:
            at = pl.ds(64 * k + step, 8, stride=8)
            c = courant_t[at, :]
            u = (source_t[at, :] + flux[k]) * (1.0 / (1.0 + c))
            source_t[at, :] = u
            flux[k] = c * u
    source[...] = source_t[...].T
    x = jnp.concatenate([own[pl.ds(16, RING, stride=SENT), :], far_maps[...]], 0)
    low = lanes(x.shape) < 64
    turned = pltpu.roll(x, 64, 1)
    rest_g = jnp.where(low, x, turned)
    rest_o = jnp.where(low, turned, x)
    for stride in (1, 2, 4, 8, 16):
        rest_o = rest_g * pltpu.roll(rest_o, stride, 0) + rest_o
        rest_g = rest_g * pltpu.roll(rest_g, stride, 0)
    rest = pltpu.roll(rest_o / (1.0 - rest_g), 1, 0)
    wrap = jnp.where(half == 0, rest[:1], rest[RING : RING + 1])
    lane = lanes((1, 128))
    areas = area[...]
    mine = lane // 64 == parity
    in_slab = polar & (lane >= start) & (lane < start + SLAB)
    weighted = jnp.where(mine & ~in_slab, areas, 0.0) * wrap
    weighted = jnp.sum(weighted, axis=1, keepdims=True)
    slab_area = jnp.sum(jnp.where(polar & (lane == start + row), areas, 0.0), axis=1, keepdims=True)
    loops = pltpu.roll(inflow, (4 * parity + 128 - 64 * half) % 128, 1) * slab_area
    sums = jnp.where(lane == row, weighted, 0.0)
    sums = sums + jnp.where((lane >= 4 * parity) & (lane < 4 * parity + 4), loops, 0.0)
    total = jnp.sum(areas, axis=1, keepdims=True)
    sums = jnp.where(lane == 8, jnp.where(ring == 0, total, 0.0), sums)
    zeros = jnp.zeros((BACK - 8, 128), jnp.float32)
    for d in range(RING):
        for side in range(2):
            back[d, pl.ds(4 * side, 4), :] = source[pl.ds(4 * d, 4), pl.ds(side * 128, 128)]
        back[d, pl.ds(8, BACK - 8), :] = zeros
        back[d, pl.ds(8, 1), :] = rest[d : d + 1]
        back[d, pl.ds(9, 1), :] = sums


def solve(hops, area, own, far_slab, far_maps):
    f32 = jnp.float32
    return pl.pallas_call(
        solve_kernel,
        out_shape=pltpu.VMEM((RING, BACK, 128), f32),
        in_specs=[SMEM] + [VMEM] * 4,
        out_specs=VMEM,
        scratch_shapes=[pltpu.VMEM((ROWS, CELLS), f32)] * 2 + [pltpu.VMEM((CELLS, ROWS), f32)] * 2,
        name="solve",
    )(hops, area, *in_vmem(own, far_slab, far_maps))


def spread_kernel(got, sums):
    total = jnp.sum(got[pl.ds(9, RING, stride=BACK), :], axis=0, keepdims=True)
    for i in range(sums.shape[0]):
        sums[i] = total


def spread(got, lats):
    return pl.pallas_call(
        spread_kernel,
        out_shape=jax.ShapeDtypeStruct((lats, 1, 128), jnp.float32),
        in_specs=[VMEM],
        out_specs=VMEM,
        name="spread",
    )(*in_vmem(got))


def finish_kernel(source_t, courant_t, entries, got, updated, updated_t):
    low = lanes((LEVELS, ROWS)) < 64
    even = got[pl.ds(8, LEVELS, stride=2 * BACK), :]
    odd = got[pl.ds(8 + BACK, LEVELS, stride=2 * BACK), :]
    inflow = jnp.where(low, even, odd)
    flux = [inflow] + [entries[2 * k] * inflow + entries[2 * k + 1] for k in range(1, SEGMENTS)]
    for step in range(STEPS):
        for k in range(SEGMENTS):
            at = pl.ds(LEVELS * (STEPS * k + step), LEVELS)
            c = courant_t[at, :]
            u = (source_t[at, :] + flux[k]) * (1.0 / (1.0 + c))
            updated_t[at, :] = u
            flux[k] = c * u
    for l in range(LEVELS):
        updated[l] = updated_t[pl.ds(l, CELLS, stride=LEVELS), :].T
    polar, start = polar_start()

    @pl.when(polar)
    def _():
        rows = pl.ds(start, SLAB)
        for l in range(LEVELS):
            for side in range(2):
                at = (l // 4) * BACK + 4 * side + l % 4
                updated[l, rows, pl.ds(side * 128, 128)] = got[pl.ds(at, SLAB, stride=2 * BACK), :]


def finish(source_t, courant_t, entries, got):
    return pl.pallas_call(
        finish_kernel,
        out_shape=jax.ShapeDtypeStruct((LEVELS, ROWS, CELLS), jnp.float32),
        in_specs=[VMEM] * 4,
        out_specs=VMEM,
        scratch_shapes=[pltpu.VMEM((CELLS * LEVELS, ROWS), jnp.float32)],
        name="finish",
    )(*in_vmem(source_t, courant_t, entries, got))


def mean_kernel(sums, mean):
    total = sums[0]
    for i in range(1, sums.shape[0]):
        total = total + sums[i]
    area = jnp.sum(jnp.where(lanes((1, 128)) == 8, total, 0.0), axis=1, keepdims=True)
    mean[...] = (total / area)[0, :LEVELS]


def mean(sums):
    return pl.pallas_call(
        mean_kernel,
        out_shape=jax.ShapeDtypeStruct((LEVELS,), jnp.float32),
        in_specs=[VMEM],
        out_specs=VMEM,
        name="mean",
    )(*in_vmem(sums))


def body(tracer, courant, hop_counts, row_area):
    lats = lax.axis_size("lat")

    def across(i):
        h, rest = divmod(i, RING * lats)
        moved = rest % lats in (0, lats - 1)
        return (i, (1 - h) * RING * lats + rest if moved else i)

    sent, source_t, courant_t, entries = pack(tracer, courant)
    got = lax.all_to_all(sent, "ring", 0, 0, tiled=True)
    every = ("half", "ring", "lat")
    far_slab = lax.ppermute(got[:, :16], every, [across(i) for i in range(HALVES * RING * lats)])
    far_maps = lax.ppermute(got[:, 16], "half", [(0, 1), (1, 0)])
    back = solve(
        hop_counts,
        row_area.reshape(1, ROWS),
        got.reshape(RING * SENT, 128),
        far_slab.reshape(RING * 16, 128),
        far_maps,
    )
    back = lax.all_to_all(back, "ring", 0, 0, tiled=True).reshape(RING * BACK, 128)
    sums = lax.all_to_all(spread(back, lats), "lat", 0, 0, tiled=True)
    return finish(source_t, courant_t, entries, back), mean(sums)


def solution(mesh):
    split = Mesh(mesh.devices.reshape(HALVES, RING, -1), ("half", "ring", "lat"))
    field = P(None, "lat", ("half", "ring"))
    return jax.shard_map(
        body,
        mesh=split,
        in_specs=(field, field, P("lat"), P("lat")),
        out_specs=(field, P()),
        check_vma=False,
    )
```

```python
import jax
import jax.numpy as jnp
from jax import lax
from jax.experimental import pallas as pl
from jax.experimental.pallas import tpu as pltpu
from jax.sharding import Mesh, PartitionSpec as P

HALVES, RING, LEVELS, ROWS, CELLS, SLAB = 2, 16, 8, 128, 256, 8
SEGMENTS = 8
STEPS = CELLS // SEGMENTS
SENT = 17
BACK = 10

VMEM = pl.BlockSpec(memory_space=pltpu.VMEM)
SMEM = pl.BlockSpec(memory_space=pltpu.SMEM)


def lanes(shape):
    return lax.broadcasted_iota(jnp.int32, shape, len(shape) - 1)


def polar_start():
    lat = lax.axis_index("lat")
    last = lat == lax.axis_size("lat") - 1
    return (lat == 0) | last, pl.multiple_of(jnp.where(last, ROWS - SLAB, 0), SLAB)


def in_vmem(*arrays):
    return [pltpu.with_memory_space_constraint(x, pltpu.VMEM) for x in arrays]


def pack_kernel(tracer, courant, sent, source_t, courant_t, entries, source, factor, slab, sems):
    copies = [
        (
            pltpu.make_async_copy(tracer.at[l], source.at[l], sems.at[0, l]),
            pltpu.make_async_copy(courant.at[l], factor.at[l], sems.at[1, l]),
        )
        for l in range(LEVELS)
    ]
    for pair in copies:
        for copy in pair:
            copy.start()
    _, start = polar_start()
    for l in range(LEVELS):
        for copy in copies[l]:
            copy.wait()
        source_t[pl.ds(l, CELLS, stride=LEVELS), :] = source[l].T
        courant_t[pl.ds(l, CELLS, stride=LEVELS), :] = factor[l].T
        for side in range(2):
            across = pl.ds(128 * side, 128)
            slab[side, pl.ds(SLAB * l, SLAB), :] = source[l, pl.ds(start, SLAB), across]
            slab[2 + side, pl.ds(SLAB * l, SLAB), :] = factor[l, pl.ds(start, SLAB), across]
    growth = [jnp.ones((LEVELS, ROWS), jnp.float32)] * SEGMENTS
    offset = [jnp.zeros((LEVELS, ROWS), jnp.float32)] * SEGMENTS
    for step in range(STEPS):
        for k in range(SEGMENTS):
            at = pl.ds(LEVELS * (STEPS * k + step), LEVELS)
            c = courant_t[at, :]
            f = c * (1.0 / (1.0 + c))
            offset[k] = f * (source_t[at, :] + offset[k])
            growth[k] = growth[k] * f
    g, o = growth[0], offset[0]
    for k in range(1, SEGMENTS):
        entries[2 * k] = g
        entries[2 * k + 1] = o
        g, o = g * growth[k], growth[k] * o + offset[k]
    low = lanes((LEVELS, ROWS)) < 64
    maps = (jnp.where(low, g, pltpu.roll(o, 64, 1)), jnp.where(low, pltpu.roll(g, 64, 1), o))
    for r in range(SLAB):
        for a in range(4):
            x = slab[a, pl.ds(r, LEVELS, stride=SLAB), :]
            sent[pl.ds(SENT * 2 * r + 4 * a, 4), :] = x[:4]
            sent[pl.ds(SENT * (2 * r + 1) + 4 * a, 4), :] = x[4:]
        for parity in range(2):
            sent[pl.ds(SENT * (2 * r + parity) + 16, 1), :] = maps[parity][r : r + 1]


def pack(tracer, courant):
    f32 = jnp.float32
    return pl.pallas_call(
        pack_kernel,
        out_shape=(
            pltpu.VMEM((RING * SENT, 128), f32),
            pltpu.VMEM((CELLS * LEVELS, ROWS), f32),
            pltpu.VMEM((CELLS * LEVELS, ROWS), f32),
            pltpu.VMEM((2 * SEGMENTS, LEVELS, ROWS), f32),
        ),
        in_specs=[pl.BlockSpec(memory_space=pl.ANY)] * 2,
        out_specs=(VMEM,) * 4,
        scratch_shapes=[
            pltpu.VMEM((LEVELS, ROWS, CELLS), f32),
            pltpu.VMEM((LEVELS, ROWS, CELLS), f32),
            pltpu.VMEM((4, LEVELS * SLAB, 128), f32),
            pltpu.SemaphoreType.DMA((2, LEVELS)),
        ],
        name="pack",
    )(tracer, courant)


def solve_kernel(hops, area, own, far, far_maps, back, source, courant, source_t, courant_t):
    half = lax.axis_index("half")
    ring = lax.axis_index("ring")
    polar, start = polar_start()
    row, parity = ring // 2, ring % 2
    for d in range(HALVES * RING):
        ref, base = (own if d < RING else far), (d % RING) * SENT
        for side in range(2):
            to = pl.ds(side * 128, 128)
            source[pl.ds(4 * d, 4), to] = ref[pl.ds(base + 4 * side, 4), :]
            courant[pl.ds(4 * d, 4), to] = ref[pl.ds(base + 8 + 4 * side, 4), :]
    source_t[...] = pltpu.roll(source[...].T, 4 * hops[start + row], 1)
    courant_t[...] = courant[...].T
    parts = range(CELLS // 64)
    growth = [jnp.ones((8, ROWS), jnp.float32) for k in parts]
    offset = [jnp.zeros((8, ROWS), jnp.float32) for k in parts]
    for step in range(8):
        for k in parts:
            at = pl.ds(64 * k + step, 8, stride=8)
            c = courant_t[at, :]
            f = c * (1.0 / (1.0 + c))
            offset[k] = f * (source_t[at, :] + offset[k])
            growth[k] = growth[k] * f
    place = lax.broadcasted_iota(jnp.int32, (8, ROWS), 0)
    for stride in (1, 2, 4):
        inside = place >= stride
        for k in parts:
            offset[k] = jnp.where(inside, growth[k] * pltpu.roll(offset[k], stride, 0) + offset[k], offset[k])
            growth[k] = jnp.where(inside, growth[k] * pltpu.roll(growth[k], stride, 0), growth[k])
    g = jnp.ones((1, ROWS), jnp.float32)
    o = jnp.zeros((1, ROWS), jnp.float32)
    entry = []
    for k in parts:
        first = place == 0
        before_g = jnp.where(first, 1.0, pltpu.roll(growth[k], 1, 0))
        before_o = jnp.where(first, 0.0, pltpu.roll(offset[k], 1, 0))
        entry.append((before_g * g, before_g * o + before_o))
        g, o = g * growth[k][7:], growth[k][7:] * o + offset[k][7:]
    for stride in (4, 8, 16, 32, 64):
        o = g * pltpu.roll(o, stride, 1) + o
        g = g * pltpu.roll(g, stride, 1)
    inflow = pltpu.roll(o / (1.0 - g), 4, 1)
    flux = [entry[k][0] * inflow + entry[k][1] for k in parts]
    for step in range(8):
        for k in parts:
            at = pl.ds(64 * k + step, 8, stride=8)
            c = courant_t[at, :]
            u = (source_t[at, :] + flux[k]) * (1.0 / (1.0 + c))
            source_t[at, :] = u
            flux[k] = c * u
    source[...] = source_t[...].T
    at = pl.ds(16, RING, stride=SENT)
    x = jnp.concatenate([own[at, :], jnp.where(polar, far[at, :], far_maps[...])], 0)
    low = lanes(x.shape) < 64
    turned = pltpu.roll(x, 64, 1)
    rest_g = jnp.where(low, x, turned)
    rest_o = jnp.where(low, turned, x)
    for stride in (1, 2, 4, 8, 16):
        rest_o = rest_g * pltpu.roll(rest_o, stride, 0) + rest_o
        rest_g = rest_g * pltpu.roll(rest_g, stride, 0)
    rest = pltpu.roll(rest_o / (1.0 - rest_g), 1, 0)
    wrap = jnp.where(half == 0, rest[:1], rest[RING : RING + 1])
    lane = lanes((1, 128))
    areas = area[...]
    mine = lane // 64 == parity
    in_slab = polar & (lane >= start) & (lane < start + SLAB)
    weighted = jnp.where(mine & ~in_slab, areas, 0.0) * wrap
    weighted = jnp.sum(weighted, axis=1, keepdims=True)
    slab_area = jnp.sum(jnp.where(polar & (lane == start + row), areas, 0.0), axis=1, keepdims=True)
    loops = pltpu.roll(inflow, (4 * parity + 128 - 64 * half) % 128, 1) * slab_area
    sums = jnp.where(lane == row, weighted, 0.0)
    sums = sums + jnp.where((lane >= 4 * parity) & (lane < 4 * parity + 4), loops, 0.0)
    total = jnp.sum(areas, axis=1, keepdims=True)
    sums = jnp.where(lane == 8, jnp.where(ring == 0, total, 0.0), sums)
    for d in range(RING):
        for side in range(2):
            back[pl.ds(BACK * d + 4 * side, 4), :] = source[pl.ds(4 * d, 4), pl.ds(side * 128, 128)]
        back[pl.ds(BACK * d + 8, 1), :] = rest[d : d + 1]
        back[pl.ds(BACK * d + 9, 1), :] = sums


def solve(hops, area, own, far, far_maps):
    f32 = jnp.float32
    return pl.pallas_call(
        solve_kernel,
        out_shape=pltpu.VMEM((RING * BACK, 128), f32),
        in_specs=[SMEM] + [VMEM] * 4,
        out_specs=VMEM,
        scratch_shapes=[pltpu.VMEM((ROWS, CELLS), f32)] * 2 + [pltpu.VMEM((CELLS, ROWS), f32)] * 2,
        name="solve",
    )(hops, area, *in_vmem(own, far, far_maps))


def spread_kernel(got, sums):
    total = jnp.sum(got[pl.ds(9, RING, stride=BACK), :], axis=0, keepdims=True)
    for i in range(sums.shape[0]):
        sums[i] = total


def spread(got, lats):
    return pl.pallas_call(
        spread_kernel,
        out_shape=jax.ShapeDtypeStruct((lats, 1, 128), jnp.float32),
        in_specs=[VMEM],
        out_specs=VMEM,
        name="spread",
    )(*in_vmem(got))


def finish_kernel(source_t, courant_t, entries, got, updated, updated_t):
    low = lanes((LEVELS, ROWS)) < 64
    even = got[pl.ds(8, LEVELS, stride=2 * BACK), :]
    odd = got[pl.ds(8 + BACK, LEVELS, stride=2 * BACK), :]
    inflow = jnp.where(low, even, odd)
    flux = [inflow] + [entries[2 * k] * inflow + entries[2 * k + 1] for k in range(1, SEGMENTS)]
    for step in range(STEPS):
        for k in range(SEGMENTS):
            at = pl.ds(LEVELS * (STEPS * k + step), LEVELS)
            c = courant_t[at, :]
            u = (source_t[at, :] + flux[k]) * (1.0 / (1.0 + c))
            updated_t[at, :] = u
            flux[k] = c * u
    for l in range(LEVELS):
        updated[l] = updated_t[pl.ds(l, CELLS, stride=LEVELS), :].T
    polar, start = polar_start()

    @pl.when(polar)
    def _():
        rows = pl.ds(start, SLAB)
        for l in range(LEVELS):
            for side in range(2):
                at = (l // 4) * BACK + 4 * side + l % 4
                updated[l, rows, pl.ds(side * 128, 128)] = got[pl.ds(at, SLAB, stride=2 * BACK), :]


def finish(source_t, courant_t, entries, got):
    return pl.pallas_call(
        finish_kernel,
        out_shape=jax.ShapeDtypeStruct((LEVELS, ROWS, CELLS), jnp.float32),
        in_specs=[VMEM] * 4,
        out_specs=VMEM,
        scratch_shapes=[pltpu.VMEM((CELLS * LEVELS, ROWS), jnp.float32)],
        name="finish",
    )(*in_vmem(source_t, courant_t, entries, got))


def mean_kernel(sums, mean):
    total = sums[0]
    for i in range(1, sums.shape[0]):
        total = total + sums[i]
    area = jnp.sum(jnp.where(lanes((1, 128)) == 8, total, 0.0), axis=1, keepdims=True)
    mean[...] = (total / area)[0, :LEVELS]


def mean(sums):
    return pl.pallas_call(
        mean_kernel,
        out_shape=jax.ShapeDtypeStruct((LEVELS,), jnp.float32),
        in_specs=[VMEM],
        out_specs=VMEM,
        name="mean",
    )(*in_vmem(sums))


def exchange(rows):
    blocks = rows.reshape(RING, -1, 1, 128)
    return lax.all_to_all(blocks, "ring", 0, 0, tiled=True).reshape(rows.shape)


def body(tracer, courant, hop_counts, row_area):
    lats = lax.axis_size("lat")

    def across(polar):
        half = RING * lats
        pairs = []
        for i in range(HALVES * half):
            moved = (i % lats in (0, lats - 1)) == polar
            pairs.append((i, (i + half) % (HALVES * half) if moved else i))
        return pairs

    sent, source_t, courant_t, entries = pack(tracer, courant)
    got = exchange(sent)
    every = ("half", "ring", "lat")
    far = lax.ppermute(got, every, across(True))
    far_maps = lax.ppermute(lax.slice(got, (16, 0), (RING * SENT, 128), (SENT, 1)), every, across(False))
    back = solve(hop_counts, row_area.reshape(1, ROWS), got, far, far_maps)
    back = exchange(back)
    sums = lax.all_to_all(spread(back, lats), "lat", 0, 0, tiled=True)
    return finish(source_t, courant_t, entries, back), mean(sums)


def solution(mesh):
    split = Mesh(mesh.devices.reshape(HALVES, RING, -1), ("half", "ring", "lat"))
    field = P(None, "lat", ("half", "ring"))
    return jax.shard_map(
        body,
        mesh=split,
        in_specs=(field, field, P("lat"), P("lat")),
        out_specs=(field, P()),
        check_vma=False,
    )
```

```python
import jax
import jax.numpy as jnp
from jax import lax
from jax.experimental import pallas as pl
from jax.experimental.pallas import tpu as pltpu
from jax.sharding import Mesh, PartitionSpec as P

HALVES, RING, LEVELS, ROWS, CELLS, SLAB = 2, 16, 8, 128, 256, 8
STOPS = 7
SEGMENTS = 8
STEPS = CELLS // SEGMENTS
SENT = 17
BACK = 10

VMEM = pl.BlockSpec(memory_space=pltpu.VMEM)


def lanes(shape):
    return lax.broadcasted_iota(jnp.int32, shape, len(shape) - 1)


def polar_start():
    lat = lax.axis_index("lat")
    last = lat == lax.axis_size("lat") - 1
    return (lat == 0) | last, pl.multiple_of(jnp.where(last, ROWS - SLAB, 0), SLAB)


def in_vmem(*arrays):
    return [pltpu.with_memory_space_constraint(x, pltpu.VMEM) for x in arrays]


def pack_kernel(
    tracer, courant, hops, area, sent, source_t, courant_t, entries, hops_out, area_out, source, factor, slab, sems
):
    rows = (
        pltpu.make_async_copy(hops, hops_out, sems.at[2, 0]),
        pltpu.make_async_copy(area, area_out, sems.at[2, 1]),
    )
    copies = [
        (
            pltpu.make_async_copy(tracer.at[l], source.at[l], sems.at[0, l]),
            pltpu.make_async_copy(courant.at[l], factor.at[l], sems.at[1, l]),
        )
        for l in range(LEVELS)
    ]
    for pair in (*copies, rows):
        for copy in pair:
            copy.start()
    _, start = polar_start()
    for l in range(LEVELS):
        for copy in copies[l]:
            copy.wait()
        source_t[pl.ds(l, CELLS, stride=LEVELS), :] = source[l].T
        courant_t[pl.ds(l, CELLS, stride=LEVELS), :] = factor[l].T
        for side in range(2):
            across = pl.ds(128 * side, 128)
            slab[side, pl.ds(SLAB * l, SLAB), :] = source[l, pl.ds(start, SLAB), across]
            slab[2 + side, pl.ds(SLAB * l, SLAB), :] = factor[l, pl.ds(start, SLAB), across]
    growth = [jnp.ones((LEVELS, ROWS), jnp.float32)] * SEGMENTS
    offset = [jnp.zeros((LEVELS, ROWS), jnp.float32)] * SEGMENTS
    for step in range(STEPS):
        for k in range(SEGMENTS):
            at = pl.ds(LEVELS * (STEPS * k + step), LEVELS)
            c = courant_t[at, :]
            f = c * (1.0 / (1.0 + c))
            offset[k] = f * (source_t[at, :] + offset[k])
            growth[k] = growth[k] * f
    g, o = growth[0], offset[0]
    for k in range(1, SEGMENTS):
        entries[2 * k] = g
        entries[2 * k + 1] = o
        g, o = g * growth[k], growth[k] * o + offset[k]
    low = lanes((LEVELS, ROWS)) < 64
    maps = (jnp.where(low, g, pltpu.roll(o, 64, 1)), jnp.where(low, pltpu.roll(g, 64, 1), o))
    for r in range(SLAB):
        for a in range(4):
            x = slab[a, pl.ds(r, LEVELS, stride=SLAB), :]
            sent[pl.ds(SENT * 2 * r + 4 * a, 4), :] = x[:4]
            sent[pl.ds(SENT * (2 * r + 1) + 4 * a, 4), :] = x[4:]
        for parity in range(2):
            sent[pl.ds(SENT * (2 * r + parity) + 16, 1), :] = maps[parity][r : r + 1]
    for copy in rows:
        copy.wait()


def pack(tracer, courant, hops, area):
    f32 = jnp.float32
    return pl.pallas_call(
        pack_kernel,
        out_shape=(
            pltpu.VMEM((RING * SENT, 128), f32),
            pltpu.VMEM((CELLS * LEVELS, ROWS), f32),
            pltpu.VMEM((CELLS * LEVELS, ROWS), f32),
            pltpu.VMEM((2 * SEGMENTS, LEVELS, ROWS), f32),
            pltpu.VMEM((1, ROWS), jnp.int32),
            pltpu.VMEM((1, ROWS), f32),
        ),
        in_specs=[pl.BlockSpec(memory_space=pl.ANY)] * 4,
        out_specs=(VMEM,) * 6,
        scratch_shapes=[
            pltpu.VMEM((LEVELS, ROWS, CELLS), f32),
            pltpu.VMEM((LEVELS, ROWS, CELLS), f32),
            pltpu.VMEM((4, LEVELS * SLAB, 128), f32),
            pltpu.SemaphoreType.DMA((3, LEVELS)),
        ],
        name="pack",
    )(tracer, courant, hops, area)


def solve_kernel(hops, area, own, far, far_maps, back, source, courant, source_t, courant_t):
    half = lax.axis_index("half")
    ring = lax.axis_index("ring")
    polar, start = polar_start()
    row, parity = ring // 2, ring % 2
    for d in range(HALVES * RING):
        ref, base = (own if d < RING else far), (d % RING) * SENT
        for side in range(2):
            to = pl.ds(side * 128, 128)
            source[pl.ds(4 * d, 4), to] = ref[pl.ds(base + 4 * side, 4), :]
            courant[pl.ds(4 * d, 4), to] = ref[pl.ds(base + 8 + 4 * side, 4), :]
    lane = lanes((1, 128))
    slab_row = lane == start + row
    hop = jnp.sum(jnp.where(slab_row, hops[...].astype(jnp.float32), 0.0), axis=1, keepdims=True).astype(jnp.int32)
    shifted = source[...].T
    for bit in range(STOPS.bit_length()):
        shifted = jnp.where((hop >> bit) % 2 == 1, pltpu.roll(shifted, 4 << bit, 1), shifted)
    source_t[...] = shifted
    courant_t[...] = courant[...].T
    parts = range(CELLS // 64)
    growth = [jnp.ones((8, ROWS), jnp.float32) for k in parts]
    offset = [jnp.zeros((8, ROWS), jnp.float32) for k in parts]
    for step in range(8):
        for k in parts:
            at = pl.ds(64 * k + step, 8, stride=8)
            c = courant_t[at, :]
            f = c * (1.0 / (1.0 + c))
            offset[k] = f * (source_t[at, :] + offset[k])
            growth[k] = growth[k] * f
    place = lax.broadcasted_iota(jnp.int32, (8, ROWS), 0)
    for stride in (1, 2, 4):
        inside = place >= stride
        for k in parts:
            offset[k] = jnp.where(inside, growth[k] * pltpu.roll(offset[k], stride, 0) + offset[k], offset[k])
            growth[k] = jnp.where(inside, growth[k] * pltpu.roll(growth[k], stride, 0), growth[k])
    g = jnp.ones((1, ROWS), jnp.float32)
    o = jnp.zeros((1, ROWS), jnp.float32)
    entry = []
    for k in parts:
        first = place == 0
        before_g = jnp.where(first, 1.0, pltpu.roll(growth[k], 1, 0))
        before_o = jnp.where(first, 0.0, pltpu.roll(offset[k], 1, 0))
        entry.append((before_g * g, before_g * o + before_o))
        g, o = g * growth[k][7:], growth[k][7:] * o + offset[k][7:]
    for stride in (4, 8, 16, 32, 64):
        o = g * pltpu.roll(o, stride, 1) + o
        g = g * pltpu.roll(g, stride, 1)
    inflow = pltpu.roll(o / (1.0 - g), 4, 1)
    flux = [entry[k][0] * inflow + entry[k][1] for k in parts]
    for step in range(8):
        for k in parts:
            at = pl.ds(64 * k + step, 8, stride=8)
            c = courant_t[at, :]
            u = (source_t[at, :] + flux[k]) * (1.0 / (1.0 + c))
            source_t[at, :] = u
            flux[k] = c * u
    source[...] = source_t[...].T
    at = pl.ds(16, RING, stride=SENT)
    x = jnp.concatenate([own[at, :], jnp.where(polar, far[at, :], far_maps[...])], 0)
    low = lanes(x.shape) < 64
    turned = pltpu.roll(x, 64, 1)
    rest_g = jnp.where(low, x, turned)
    rest_o = jnp.where(low, turned, x)
    for stride in (1, 2, 4, 8, 16):
        rest_o = rest_g * pltpu.roll(rest_o, stride, 0) + rest_o
        rest_g = rest_g * pltpu.roll(rest_g, stride, 0)
    rest = pltpu.roll(rest_o / (1.0 - rest_g), 1, 0)
    wrap = jnp.where(half == 0, rest[:1], rest[RING : RING + 1])
    areas = area[...]
    mine = lane // 64 == parity
    in_slab = polar & (lane >= start) & (lane < start + SLAB)
    weighted = jnp.where(mine & ~in_slab, areas, 0.0) * wrap
    weighted = jnp.sum(weighted, axis=1, keepdims=True)
    slab_area = jnp.sum(jnp.where(polar & slab_row, areas, 0.0), axis=1, keepdims=True)
    loops = pltpu.roll(inflow, (4 * parity + 128 - 64 * half) % 128, 1) * slab_area
    sums = jnp.where(lane == row, weighted, 0.0)
    sums = sums + jnp.where((lane >= 4 * parity) & (lane < 4 * parity + 4), loops, 0.0)
    total = jnp.sum(areas, axis=1, keepdims=True)
    sums = jnp.where(lane == 8, jnp.where(ring == 0, total, 0.0), sums)
    for d in range(RING):
        for side in range(2):
            back[pl.ds(BACK * d + 4 * side, 4), :] = source[pl.ds(4 * d, 4), pl.ds(side * 128, 128)]
        back[pl.ds(BACK * d + 8, 1), :] = rest[d : d + 1]
        back[pl.ds(BACK * d + 9, 1), :] = sums


def solve(hops, area, own, far, far_maps):
    f32 = jnp.float32
    return pl.pallas_call(
        solve_kernel,
        out_shape=pltpu.VMEM((RING * BACK, 128), f32),
        in_specs=[VMEM] * 5,
        out_specs=VMEM,
        scratch_shapes=[pltpu.VMEM((ROWS, CELLS), f32)] * 2 + [pltpu.VMEM((CELLS, ROWS), f32)] * 2,
        name="solve",
    )(*in_vmem(hops, area, own, far, far_maps))


def spread_kernel(got, sums):
    total = jnp.sum(got[pl.ds(9, RING, stride=BACK), :], axis=0, keepdims=True)
    for i in range(sums.shape[0]):
        sums[i] = total


def spread(got, lats):
    return pl.pallas_call(
        spread_kernel,
        out_shape=pltpu.VMEM((lats, 1, 128), jnp.float32),
        in_specs=[VMEM],
        out_specs=VMEM,
        name="spread",
    )(*in_vmem(got))


def finish_kernel(source_t, courant_t, entries, got, sums, updated, mean, updated_t, level, sems):
    low = lanes((LEVELS, ROWS)) < 64
    even = got[pl.ds(8, LEVELS, stride=2 * BACK), :]
    odd = got[pl.ds(8 + BACK, LEVELS, stride=2 * BACK), :]
    inflow = jnp.where(low, even, odd)
    flux = [inflow] + [entries[2 * k] * inflow + entries[2 * k + 1] for k in range(1, SEGMENTS)]
    for step in range(STEPS):
        for k in range(SEGMENTS):
            at = pl.ds(LEVELS * (STEPS * k + step), LEVELS)
            c = courant_t[at, :]
            u = (source_t[at, :] + flux[k]) * (1.0 / (1.0 + c))
            updated_t[at, :] = u
            flux[k] = c * u
    polar, start = polar_start()
    rows = pl.ds(start, SLAB)
    copies = []
    for l in range(LEVELS):
        level[l] = updated_t[pl.ds(l, CELLS, stride=LEVELS), :].T
        for side in range(2):
            to = pl.ds(side * 128, 128)
            at = (l // 4) * BACK + 4 * side + l % 4
            solved = got[pl.ds(at, SLAB, stride=2 * BACK), :]
            level[l, rows, to] = jnp.where(polar, solved, level[l, rows, to])
        copies.append(pltpu.make_async_copy(level.at[l], updated.at[l], sems.at[l]))
        copies[l].start()
    total = sums[0]
    for i in range(1, sums.shape[0]):
        total = total + sums[i]
    area = jnp.sum(jnp.where(lanes((1, 128)) == 8, total, 0.0), axis=1, keepdims=True)
    mean[...] = (total / area)[0, :LEVELS]
    for copy in copies:
        copy.wait()


def finish(source_t, courant_t, entries, got, sums):
    f32 = jnp.float32
    return pl.pallas_call(
        finish_kernel,
        out_shape=(
            jax.ShapeDtypeStruct((LEVELS, ROWS, CELLS), f32),
            jax.ShapeDtypeStruct((LEVELS,), f32),
        ),
        in_specs=[VMEM] * 5,
        out_specs=(pl.BlockSpec(memory_space=pl.ANY), VMEM),
        scratch_shapes=[
            pltpu.VMEM((CELLS * LEVELS, ROWS), f32),
            pltpu.VMEM((LEVELS, ROWS, CELLS), f32),
            pltpu.SemaphoreType.DMA((LEVELS,)),
        ],
        name="finish",
    )(*in_vmem(source_t, courant_t, entries, got, sums))


def exchange(rows):
    blocks = rows.reshape(RING, -1, 1, 128)
    return lax.all_to_all(blocks, "ring", 0, 0, tiled=True).reshape(rows.shape)


def body(tracer, courant, hop_counts, row_area):
    lats = lax.axis_size("lat")

    def across(polar):
        half = RING * lats
        pairs = []
        for i in range(HALVES * half):
            moved = (i % lats in (0, lats - 1)) == polar
            pairs.append((i, (i + half) % (HALVES * half) if moved else i))
        return pairs

    hops, area = hop_counts.reshape(1, ROWS), row_area.reshape(1, ROWS)
    sent, source_t, courant_t, entries, hops, area = pack(tracer, courant, hops, area)
    got = exchange(sent)
    every = ("half", "ring", "lat")
    far = lax.ppermute(got, every, across(True))
    far_maps = lax.ppermute(lax.slice(got, (16, 0), (RING * SENT, 128), (SENT, 1)), every, across(False))
    back = solve(hops, area, got, far, far_maps)
    back = exchange(back)
    sums = lax.all_to_all(spread(back, lats), "lat", 0, 0, tiled=True)
    return finish(source_t, courant_t, entries, back, sums)


def solution(mesh):
    split = Mesh(mesh.devices.reshape(HALVES, RING, -1), ("half", "ring", "lat"))
    field = P(None, "lat", ("half", "ring"))
    return jax.shard_map(
        body,
        mesh=split,
        in_specs=(field, field, P("lat"), P("lat")),
        out_specs=(field, P()),
        check_vma=False,
    )
```

```python
import jax
import jax.numpy as jnp
from jax import lax
from jax.experimental import pallas as pl
from jax.experimental.pallas import tpu as pltpu
from jax.sharding import Mesh, PartitionSpec as P

HALVES, RING, LEVELS, ROWS, CELLS, SLAB = 2, 16, 8, 128, 256, 8
STOPS = 7
SEGMENTS = 8
STEPS = CELLS // SEGMENTS
SENT = 17
BACK = 10

VMEM = pl.BlockSpec(memory_space=pltpu.VMEM)


def lanes(shape):
    return lax.broadcasted_iota(jnp.int32, shape, len(shape) - 1)


def polar_start():
    lat = lax.axis_index("lat")
    last = lat == lax.axis_size("lat") - 1
    return (lat == 0) | last, pl.multiple_of(jnp.where(last, ROWS - SLAB, 0), SLAB)


def in_vmem(*arrays):
    return [pltpu.with_memory_space_constraint(x, pltpu.VMEM) for x in arrays]


def pack_kernel(
    tracer, courant, hops, area, sent, source_t, courant_t, entries, hops_out, area_out, source, factor, slab, sems
):
    rows = (
        pltpu.make_async_copy(hops, hops_out, sems.at[2, 0]),
        pltpu.make_async_copy(area, area_out, sems.at[2, 1]),
    )
    copies = [
        (
            pltpu.make_async_copy(tracer.at[l], source.at[l], sems.at[0, l]),
            pltpu.make_async_copy(courant.at[l], factor.at[l], sems.at[1, l]),
        )
        for l in range(LEVELS)
    ]
    for pair in (*copies, rows):
        for copy in pair:
            copy.start()
    _, start = polar_start()
    for l in range(LEVELS):
        for copy in copies[l]:
            copy.wait()
        source_t[pl.ds(l, CELLS, stride=LEVELS), :] = source[l].T
        courant_t[pl.ds(l, CELLS, stride=LEVELS), :] = factor[l].T
        for side in range(2):
            across = pl.ds(128 * side, 128)
            slab[side, pl.ds(SLAB * l, SLAB), :] = source[l, pl.ds(start, SLAB), across]
            slab[2 + side, pl.ds(SLAB * l, SLAB), :] = factor[l, pl.ds(start, SLAB), across]
    growth = [jnp.ones((LEVELS, ROWS), jnp.float32)] * SEGMENTS
    offset = [jnp.zeros((LEVELS, ROWS), jnp.float32)] * SEGMENTS
    for step in range(STEPS):
        for k in range(SEGMENTS):
            at = pl.ds(LEVELS * (STEPS * k + step), LEVELS)
            c = courant_t[at, :]
            f = c * (1.0 / (1.0 + c))
            offset[k] = f * (source_t[at, :] + offset[k])
            growth[k] = growth[k] * f
    g, o = growth[0], offset[0]
    for k in range(1, SEGMENTS):
        entries[2 * k] = g
        entries[2 * k + 1] = o
        g, o = g * growth[k], growth[k] * o + offset[k]
    low = lanes((LEVELS, ROWS)) < 64
    maps = (jnp.where(low, g, pltpu.roll(o, 64, 1)), jnp.where(low, pltpu.roll(g, 64, 1), o))
    for half in range(HALVES):
        for r in range(SLAB):
            even = SENT * (RING * half + 2 * r)
            for a in range(4):
                x = slab[a, pl.ds(r, LEVELS, stride=SLAB), :]
                sent[pl.ds(even + 4 * a, 4), :] = x[:4]
                sent[pl.ds(even + SENT + 4 * a, 4), :] = x[4:]
            for parity in range(2):
                sent[pl.ds(even + SENT * parity + 16, 1), :] = maps[parity][r : r + 1]
    for copy in rows:
        copy.wait()


def pack(tracer, courant, hops, area):
    f32 = jnp.float32
    return pl.pallas_call(
        pack_kernel,
        out_shape=(
            pltpu.VMEM((HALVES * RING * SENT, 128), f32),
            pltpu.VMEM((CELLS * LEVELS, ROWS), f32),
            pltpu.VMEM((CELLS * LEVELS, ROWS), f32),
            pltpu.VMEM((2 * SEGMENTS, LEVELS, ROWS), f32),
            pltpu.VMEM((1, ROWS), jnp.int32),
            pltpu.VMEM((1, ROWS), f32),
        ),
        in_specs=[pl.BlockSpec(memory_space=pl.ANY)] * 4,
        out_specs=(VMEM,) * 6,
        scratch_shapes=[
            pltpu.VMEM((LEVELS, ROWS, CELLS), f32),
            pltpu.VMEM((LEVELS, ROWS, CELLS), f32),
            pltpu.VMEM((4, LEVELS * SLAB, 128), f32),
            pltpu.SemaphoreType.DMA((3, LEVELS)),
        ],
        name="pack",
    )(tracer, courant, hops, area)


def solve_kernel(hops, area, got, back, source, courant, source_t, courant_t):
    half = lax.axis_index("half")
    ring = lax.axis_index("ring")
    polar, start = polar_start()
    row, parity = ring // 2, ring % 2
    for d in range(HALVES * RING):
        for side in range(2):
            to = pl.ds(side * 128, 128)
            source[pl.ds(4 * d, 4), to] = got[pl.ds(SENT * d + 4 * side, 4), :]
            courant[pl.ds(4 * d, 4), to] = got[pl.ds(SENT * d + 8 + 4 * side, 4), :]
    lane = lanes((1, 128))
    slab_row = lane == start + row
    hop = jnp.sum(jnp.where(slab_row, hops[...].astype(jnp.float32), 0.0), axis=1, keepdims=True).astype(jnp.int32)
    shifted = source[...].T
    for bit in range(STOPS.bit_length()):
        shifted = jnp.where((hop >> bit) % 2 == 1, pltpu.roll(shifted, 4 << bit, 1), shifted)
    source_t[...] = shifted
    courant_t[...] = courant[...].T
    parts = range(CELLS // 64)
    growth = [jnp.ones((8, ROWS), jnp.float32) for k in parts]
    offset = [jnp.zeros((8, ROWS), jnp.float32) for k in parts]
    for step in range(8):
        for k in parts:
            at = pl.ds(64 * k + step, 8, stride=8)
            c = courant_t[at, :]
            f = c * (1.0 / (1.0 + c))
            offset[k] = f * (source_t[at, :] + offset[k])
            growth[k] = growth[k] * f
    place = lax.broadcasted_iota(jnp.int32, (8, ROWS), 0)
    for stride in (1, 2, 4):
        inside = place >= stride
        for k in parts:
            offset[k] = jnp.where(inside, growth[k] * pltpu.roll(offset[k], stride, 0) + offset[k], offset[k])
            growth[k] = jnp.where(inside, growth[k] * pltpu.roll(growth[k], stride, 0), growth[k])
    g = jnp.ones((1, ROWS), jnp.float32)
    o = jnp.zeros((1, ROWS), jnp.float32)
    entry = []
    for k in parts:
        first = place == 0
        before_g = jnp.where(first, 1.0, pltpu.roll(growth[k], 1, 0))
        before_o = jnp.where(first, 0.0, pltpu.roll(offset[k], 1, 0))
        entry.append((before_g * g, before_g * o + before_o))
        g, o = g * growth[k][7:], growth[k][7:] * o + offset[k][7:]
    for stride in (4, 8, 16, 32, 64):
        o = g * pltpu.roll(o, stride, 1) + o
        g = g * pltpu.roll(g, stride, 1)
    inflow = pltpu.roll(o / (1.0 - g), 4, 1)
    flux = [entry[k][0] * inflow + entry[k][1] for k in parts]
    for step in range(8):
        for k in parts:
            at = pl.ds(64 * k + step, 8, stride=8)
            c = courant_t[at, :]
            u = (source_t[at, :] + flux[k]) * (1.0 / (1.0 + c))
            source_t[at, :] = u
            flux[k] = c * u
    source[...] = source_t[...].T
    x = got[pl.ds(16, HALVES * RING, stride=SENT), :]
    low = lanes(x.shape) < 64
    turned = pltpu.roll(x, 64, 1)
    rest_g = jnp.where(low, x, turned)
    rest_o = jnp.where(low, turned, x)
    for stride in (1, 2, 4, 8, 16):
        rest_o = rest_g * pltpu.roll(rest_o, stride, 0) + rest_o
        rest_g = rest_g * pltpu.roll(rest_g, stride, 0)
    rest = pltpu.roll(rest_o / (1.0 - rest_g), 1, 0)
    areas = area[...]
    mine = lane // 64 == parity
    in_slab = polar & (lane >= start) & (lane < start + SLAB)
    weighted = jnp.where(mine & ~in_slab, areas, 0.0) * rest[:1]
    weighted = jnp.sum(weighted, axis=1, keepdims=True)
    slab_area = jnp.sum(jnp.where(polar & slab_row, areas, 0.0), axis=1, keepdims=True)
    loops = pltpu.roll(inflow, 4 * parity, 1) * slab_area
    sums = jnp.where(lane == row, weighted, 0.0)
    sums = sums + jnp.where((lane >= 4 * parity) & (lane < 4 * parity + 4), loops, 0.0)
    total = jnp.sum(areas, axis=1, keepdims=True)
    sums = jnp.where(lane == 8, jnp.where(ring == 0, total, 0.0), sums)
    for d in range(RING):
        for side in range(2):
            to = pl.ds(side * 128, 128)
            solved = [source[pl.ds(4 * (d + first), 4), to] for first in (0, RING)]
            back[pl.ds(BACK * d + 4 * side, 4), :] = jnp.where(half == 0, *solved)
        back[pl.ds(BACK * d + 8, 1), :] = jnp.where(half == 0, rest[d : d + 1], rest[d + RING : d + RING + 1])
        back[pl.ds(BACK * d + 9, 1), :] = sums


def solve(hops, area, got):
    f32 = jnp.float32
    return pl.pallas_call(
        solve_kernel,
        out_shape=pltpu.VMEM((RING * BACK, 128), f32),
        in_specs=[VMEM] * 3,
        out_specs=VMEM,
        scratch_shapes=[pltpu.VMEM((ROWS, CELLS), f32)] * 2 + [pltpu.VMEM((CELLS, ROWS), f32)] * 2,
        name="solve",
    )(*in_vmem(hops, area, got))


def spread_kernel(got, sums):
    total = jnp.sum(got[pl.ds(9, RING, stride=BACK), :], axis=0, keepdims=True)
    for i in range(sums.shape[0]):
        sums[i] = total


def spread(got, lats):
    return pl.pallas_call(
        spread_kernel,
        out_shape=jax.ShapeDtypeStruct((lats, 1, 128), jnp.float32),
        in_specs=[VMEM],
        out_specs=VMEM,
        name="spread",
    )(*in_vmem(got))


def mean_kernel(sums, mean):
    total = sums[0]
    for i in range(1, sums.shape[0]):
        total = total + sums[i]
    area = jnp.sum(jnp.where(lanes((1, 128)) == 8, total, 0.0), axis=1, keepdims=True)
    mean[...] = (total / area)[0, :LEVELS]


def mean(sums):
    return pl.pallas_call(
        mean_kernel,
        out_shape=jax.ShapeDtypeStruct((LEVELS,), jnp.float32),
        in_specs=[VMEM],
        out_specs=VMEM,
        name="mean",
    )(*in_vmem(sums))


def finish_kernel(source_t, courant_t, entries, got, updated, updated_t, level, sems):
    low = lanes((LEVELS, ROWS)) < 64
    even = got[pl.ds(8, LEVELS, stride=2 * BACK), :]
    odd = got[pl.ds(8 + BACK, LEVELS, stride=2 * BACK), :]
    inflow = jnp.where(low, even, odd)
    flux = [inflow] + [entries[2 * k] * inflow + entries[2 * k + 1] for k in range(1, SEGMENTS)]
    for step in range(STEPS):
        for k in range(SEGMENTS):
            at = pl.ds(LEVELS * (STEPS * k + step), LEVELS)
            c = courant_t[at, :]
            u = (source_t[at, :] + flux[k]) * (1.0 / (1.0 + c))
            updated_t[at, :] = u
            flux[k] = c * u
    polar, start = polar_start()
    rows = pl.ds(start, SLAB)
    copies = []
    for l in range(LEVELS):
        level[l] = updated_t[pl.ds(l, CELLS, stride=LEVELS), :].T
        for side in range(2):
            to = pl.ds(side * 128, 128)
            at = (l // 4) * BACK + 4 * side + l % 4
            solved = got[pl.ds(at, SLAB, stride=2 * BACK), :]
            level[l, rows, to] = jnp.where(polar, solved, level[l, rows, to])
        copies.append(pltpu.make_async_copy(level.at[l], updated.at[l], sems.at[l]))
        copies[l].start()
    for copy in copies:
        copy.wait()


def finish(source_t, courant_t, entries, got):
    f32 = jnp.float32
    return pl.pallas_call(
        finish_kernel,
        out_shape=jax.ShapeDtypeStruct((LEVELS, ROWS, CELLS), f32),
        in_specs=[VMEM] * 4,
        out_specs=pl.BlockSpec(memory_space=pl.ANY),
        scratch_shapes=[
            pltpu.VMEM((CELLS * LEVELS, ROWS), f32),
            pltpu.VMEM((LEVELS, ROWS, CELLS), f32),
            pltpu.SemaphoreType.DMA((LEVELS,)),
        ],
        name="finish",
    )(*in_vmem(source_t, courant_t, entries, got))


def exchange(rows, axes):
    blocks = rows.reshape(lax.axis_size(axes), -1, 1, 128)
    return lax.all_to_all(blocks, axes, 0, 0, tiled=True).reshape(rows.shape)


def body(tracer, courant, hop_counts, row_area):
    hops, area = hop_counts.reshape(1, ROWS), row_area.reshape(1, ROWS)
    sent, source_t, courant_t, entries, hops, area = pack(tracer, courant, hops, area)
    got = exchange(sent, ("half", "ring"))
    back = exchange(solve(hops, area, got), "ring")
    sums = lax.all_to_all(spread(back, lax.axis_size("lat")), "lat", 0, 0, tiled=True)
    return finish(source_t, courant_t, entries, back), mean(sums)


def solution(mesh):
    split = Mesh(mesh.devices.reshape(HALVES, RING, -1), ("half", "ring", "lat"))
    field = P(None, "lat", ("half", "ring"))
    return jax.shard_map(
        body,
        mesh=split,
        in_specs=(field, field, P("lat"), P("lat")),
        out_specs=(field, P()),
        check_vma=False,
    )
```

```python
import jax
import jax.numpy as jnp
from jax import lax
from jax.experimental import pallas as pl
from jax.experimental.pallas import tpu as pltpu
from jax.sharding import Mesh, PartitionSpec as P

HALVES, RING, LEVELS, ROWS, CELLS, SLAB = 2, 16, 8, 128, 256, 8
STOPS = 7
SEGMENTS = 8
STEPS = CELLS // SEGMENTS
SENT = 17
BACK = 10

VMEM = pl.BlockSpec(memory_space=pltpu.VMEM)


def lanes(shape):
    return lax.broadcasted_iota(jnp.int32, shape, len(shape) - 1)


def polar_start():
    lat = lax.axis_index("lat")
    last = lat == lax.axis_size("lat") - 1
    return (lat == 0) | last, pl.multiple_of(jnp.where(last, ROWS - SLAB, 0), SLAB)


def in_vmem(*arrays):
    return [pltpu.with_memory_space_constraint(x, pltpu.VMEM) for x in arrays]


def pack_kernel(
    tracer, courant, hops, area, sent, source_t, courant_t, entries, hops_out, area_out, source, factor, slab, sems
):
    rows = (
        pltpu.make_async_copy(hops, hops_out, sems.at[2, 0]),
        pltpu.make_async_copy(area, area_out, sems.at[2, 1]),
    )
    copies = [
        (
            pltpu.make_async_copy(tracer.at[l], source.at[l], sems.at[0, l]),
            pltpu.make_async_copy(courant.at[l], factor.at[l], sems.at[1, l]),
        )
        for l in range(LEVELS)
    ]
    for pair in (*copies, rows):
        for copy in pair:
            copy.start()
    _, start = polar_start()
    for l in range(LEVELS):
        for copy in copies[l]:
            copy.wait()
        source_t[pl.ds(l, CELLS, stride=LEVELS), :] = source[l].T
        courant_t[pl.ds(l, CELLS, stride=LEVELS), :] = factor[l].T
        for side in range(2):
            across = pl.ds(128 * side, 128)
            slab[side, pl.ds(SLAB * l, SLAB), :] = source[l, pl.ds(start, SLAB), across]
            slab[2 + side, pl.ds(SLAB * l, SLAB), :] = factor[l, pl.ds(start, SLAB), across]
    growth = [jnp.ones((LEVELS, ROWS), jnp.float32)] * SEGMENTS
    offset = [jnp.zeros((LEVELS, ROWS), jnp.float32)] * SEGMENTS
    for step in range(STEPS):
        for k in range(SEGMENTS):
            at = pl.ds(LEVELS * (STEPS * k + step), LEVELS)
            c = courant_t[at, :]
            f = c * (1.0 / (1.0 + c))
            offset[k] = f * (source_t[at, :] + offset[k])
            growth[k] = growth[k] * f
    g, o = growth[0], offset[0]
    for k in range(1, SEGMENTS):
        entries[2 * k] = g
        entries[2 * k + 1] = o
        g, o = g * growth[k], growth[k] * o + offset[k]
    low = lanes((LEVELS, ROWS)) < 64
    maps = (jnp.where(low, g, pltpu.roll(o, 64, 1)), jnp.where(low, pltpu.roll(g, 64, 1), o))
    for r in range(SLAB):
        for a in range(4):
            x = slab[a, pl.ds(r, LEVELS, stride=SLAB), :]
            sent[pl.ds(SENT * 2 * r + 4 * a, 4), :] = x[:4]
            sent[pl.ds(SENT * (2 * r + 1) + 4 * a, 4), :] = x[4:]
        for parity in range(2):
            sent[pl.ds(SENT * (2 * r + parity) + 16, 1), :] = maps[parity][r : r + 1]
    for copy in rows:
        copy.wait()


def pack(tracer, courant, hops, area):
    f32 = jnp.float32
    return pl.pallas_call(
        pack_kernel,
        out_shape=(
            pltpu.VMEM((RING * SENT, 128), f32),
            pltpu.VMEM((CELLS * LEVELS, ROWS), f32),
            pltpu.VMEM((CELLS * LEVELS, ROWS), f32),
            pltpu.VMEM((2 * SEGMENTS, LEVELS, ROWS), f32),
            pltpu.VMEM((1, ROWS), jnp.int32),
            pltpu.VMEM((1, ROWS), f32),
        ),
        in_specs=[pl.BlockSpec(memory_space=pl.ANY)] * 4,
        out_specs=(VMEM,) * 6,
        scratch_shapes=[
            pltpu.VMEM((LEVELS, ROWS, CELLS), f32),
            pltpu.VMEM((LEVELS, ROWS, CELLS), f32),
            pltpu.VMEM((4, LEVELS * SLAB, 128), f32),
            pltpu.SemaphoreType.DMA((3, LEVELS)),
        ],
        name="pack",
    )(tracer, courant, hops, area)


def solve_kernel(hops, area, own, far, far_maps, back, source, courant, source_t, courant_t):
    half = lax.axis_index("half")
    ring = lax.axis_index("ring")
    polar, start = polar_start()
    row, parity = ring // 2, ring % 2
    for d in range(HALVES * RING):
        ref, base = (own if d < RING else far), (d % RING) * SENT
        for side in range(2):
            to = pl.ds(side * 128, 128)
            source[pl.ds(4 * d, 4), to] = ref[pl.ds(base + 4 * side, 4), :]
            courant[pl.ds(4 * d, 4), to] = ref[pl.ds(base + 8 + 4 * side, 4), :]
    lane = lanes((1, 128))
    slab_row = lane == start + row
    hop = jnp.sum(jnp.where(slab_row, hops[...].astype(jnp.float32), 0.0), axis=1, keepdims=True).astype(jnp.int32)
    shifted = source[...].T
    for bit in range(STOPS.bit_length()):
        shifted = jnp.where((hop >> bit) % 2 == 1, pltpu.roll(shifted, 4 << bit, 1), shifted)
    source_t[...] = shifted
    courant_t[...] = courant[...].T
    parts = range(CELLS // 64)
    growth = [jnp.ones((8, ROWS), jnp.float32) for k in parts]
    offset = [jnp.zeros((8, ROWS), jnp.float32) for k in parts]
    for step in range(8):
        for k in parts:
            at = pl.ds(64 * k + step, 8, stride=8)
            c = courant_t[at, :]
            f = c * (1.0 / (1.0 + c))
            offset[k] = f * (source_t[at, :] + offset[k])
            growth[k] = growth[k] * f
    place = lax.broadcasted_iota(jnp.int32, (8, ROWS), 0)
    for stride in (1, 2, 4):
        inside = place >= stride
        for k in parts:
            offset[k] = jnp.where(inside, growth[k] * pltpu.roll(offset[k], stride, 0) + offset[k], offset[k])
            growth[k] = jnp.where(inside, growth[k] * pltpu.roll(growth[k], stride, 0), growth[k])
    g = jnp.ones((1, ROWS), jnp.float32)
    o = jnp.zeros((1, ROWS), jnp.float32)
    entry = []
    for k in parts:
        first = place == 0
        before_g = jnp.where(first, 1.0, pltpu.roll(growth[k], 1, 0))
        before_o = jnp.where(first, 0.0, pltpu.roll(offset[k], 1, 0))
        entry.append((before_g * g, before_g * o + before_o))
        g, o = g * growth[k][7:], growth[k][7:] * o + offset[k][7:]
    for stride in (4, 8, 16, 32, 64):
        o = g * pltpu.roll(o, stride, 1) + o
        g = g * pltpu.roll(g, stride, 1)
    inflow = pltpu.roll(o / (1.0 - g), 4, 1)
    flux = [entry[k][0] * inflow + entry[k][1] for k in parts]
    for step in range(8):
        for k in parts:
            at = pl.ds(64 * k + step, 8, stride=8)
            c = courant_t[at, :]
            u = (source_t[at, :] + flux[k]) * (1.0 / (1.0 + c))
            source_t[at, :] = u
            flux[k] = c * u
    source[...] = source_t[...].T
    at = pl.ds(16, RING, stride=SENT)
    x = jnp.concatenate([own[at, :], jnp.where(polar, far[at, :], far_maps[...])], 0)
    low = lanes(x.shape) < 64
    turned = pltpu.roll(x, 64, 1)
    rest_g = jnp.where(low, x, turned)
    rest_o = jnp.where(low, turned, x)
    for stride in (1, 2, 4, 8, 16):
        rest_o = rest_g * pltpu.roll(rest_o, stride, 0) + rest_o
        rest_g = rest_g * pltpu.roll(rest_g, stride, 0)
    rest = pltpu.roll(rest_o / (1.0 - rest_g), 1, 0)
    wrap = jnp.where(half == 0, rest[:1], rest[RING : RING + 1])
    areas = area[...]
    mine = lane // 64 == parity
    in_slab = polar & (lane >= start) & (lane < start + SLAB)
    weighted = jnp.where(mine & ~in_slab, areas, 0.0) * wrap
    weighted = jnp.sum(weighted, axis=1, keepdims=True)
    slab_area = jnp.sum(jnp.where(polar & slab_row, areas, 0.0), axis=1, keepdims=True)
    loops = pltpu.roll(inflow, (4 * parity + 128 - 64 * half) % 128, 1) * slab_area
    sums = jnp.where(lane == row, weighted, 0.0)
    sums = sums + jnp.where((lane >= 4 * parity) & (lane < 4 * parity + 4), loops, 0.0)
    total = jnp.sum(areas, axis=1, keepdims=True)
    sums = jnp.where(lane == 8, jnp.where(ring == 0, total, 0.0), sums)
    for d in range(RING):
        for side in range(2):
            back[pl.ds(BACK * d + 4 * side, 4), :] = source[pl.ds(4 * d, 4), pl.ds(side * 128, 128)]
        back[pl.ds(BACK * d + 8, 1), :] = rest[d : d + 1]
        back[pl.ds(BACK * d + 9, 1), :] = sums


def solve(hops, area, own, far, far_maps):
    f32 = jnp.float32
    return pl.pallas_call(
        solve_kernel,
        out_shape=pltpu.VMEM((RING * BACK, 128), f32),
        in_specs=[VMEM] * 5,
        out_specs=VMEM,
        scratch_shapes=[pltpu.VMEM((ROWS, CELLS), f32)] * 2 + [pltpu.VMEM((CELLS, ROWS), f32)] * 2,
        name="solve",
    )(*in_vmem(hops, area, own, far, far_maps))


def spread_kernel(got, sums):
    total = jnp.sum(got[pl.ds(9, RING, stride=BACK), :], axis=0, keepdims=True)
    for i in range(sums.shape[0]):
        sums[i] = total


def spread(got, lats):
    return pl.pallas_call(
        spread_kernel,
        out_shape=jax.ShapeDtypeStruct((lats, 1, 128), jnp.float32),
        in_specs=[VMEM],
        out_specs=VMEM,
        name="spread",
    )(*in_vmem(got))


def mean_kernel(sums, mean):
    total = sums[0]
    for i in range(1, sums.shape[0]):
        total = total + sums[i]
    area = jnp.sum(jnp.where(lanes((1, 128)) == 8, total, 0.0), axis=1, keepdims=True)
    mean[...] = (total / area)[0, :LEVELS]


def mean(sums):
    return pl.pallas_call(
        mean_kernel,
        out_shape=jax.ShapeDtypeStruct((LEVELS,), jnp.float32),
        in_specs=[VMEM],
        out_specs=VMEM,
        name="mean",
    )(*in_vmem(sums))


def finish_kernel(source_t, courant_t, entries, got, updated, updated_t, level, sems):
    low = lanes((LEVELS, ROWS)) < 64
    even = got[pl.ds(8, LEVELS, stride=2 * BACK), :]
    odd = got[pl.ds(8 + BACK, LEVELS, stride=2 * BACK), :]
    inflow = jnp.where(low, even, odd)
    flux = [inflow] + [entries[2 * k] * inflow + entries[2 * k + 1] for k in range(1, SEGMENTS)]
    for step in range(STEPS):
        for k in range(SEGMENTS):
            at = pl.ds(LEVELS * (STEPS * k + step), LEVELS)
            c = courant_t[at, :]
            u = (source_t[at, :] + flux[k]) * (1.0 / (1.0 + c))
            updated_t[at, :] = u
            flux[k] = c * u
    polar, start = polar_start()
    rows = pl.ds(start, SLAB)
    copies = []
    for l in range(LEVELS):
        level[l] = updated_t[pl.ds(l, CELLS, stride=LEVELS), :].T
        for side in range(2):
            to = pl.ds(side * 128, 128)
            at = (l // 4) * BACK + 4 * side + l % 4
            solved = got[pl.ds(at, SLAB, stride=2 * BACK), :]
            level[l, rows, to] = jnp.where(polar, solved, level[l, rows, to])
        copies.append(pltpu.make_async_copy(level.at[l], updated.at[l], sems.at[l]))
        copies[l].start()
    for copy in copies:
        copy.wait()


def finish(source_t, courant_t, entries, got):
    f32 = jnp.float32
    return pl.pallas_call(
        finish_kernel,
        out_shape=jax.ShapeDtypeStruct((LEVELS, ROWS, CELLS), f32),
        in_specs=[VMEM] * 4,
        out_specs=pl.BlockSpec(memory_space=pl.ANY),
        scratch_shapes=[
            pltpu.VMEM((CELLS * LEVELS, ROWS), f32),
            pltpu.VMEM((LEVELS, ROWS, CELLS), f32),
            pltpu.SemaphoreType.DMA((LEVELS,)),
        ],
        name="finish",
    )(*in_vmem(source_t, courant_t, entries, got))


def exchange(rows):
    blocks = rows.reshape(RING, -1, 1, 128)
    return lax.all_to_all(blocks, "ring", 0, 0, tiled=True).reshape(rows.shape)


def body(tracer, courant, hop_counts, row_area):
    lats = lax.axis_size("lat")

    def across(polar):
        half = RING * lats
        pairs = []
        for i in range(HALVES * half):
            moved = (i % lats in (0, lats - 1)) == polar
            pairs.append((i, (i + half) % (HALVES * half) if moved else i))
        return pairs

    hops, area = hop_counts.reshape(1, ROWS), row_area.reshape(1, ROWS)
    sent, source_t, courant_t, entries, hops, area = pack(tracer, courant, hops, area)
    got = exchange(sent)
    every = ("half", "ring", "lat")
    far = lax.ppermute(got, every, across(True))
    far_maps = lax.ppermute(lax.slice(got, (16, 0), (RING * SENT, 128), (SENT, 1)), every, across(False))
    back = solve(hops, area, got, far, far_maps)
    back = exchange(back)
    sums = lax.all_to_all(spread(back, lats), "lat", 0, 0, tiled=True)
    return finish(source_t, courant_t, entries, back), mean(sums)


def solution(mesh):
    split = Mesh(mesh.devices.reshape(HALVES, RING, -1), ("half", "ring", "lat"))
    field = P(None, "lat", ("half", "ring"))
    return jax.shard_map(
        body,
        mesh=split,
        in_specs=(field, field, P("lat"), P("lat")),
        out_specs=(field, P()),
        check_vma=False,
    )
```

```python
import jax
import jax.numpy as jnp
from jax import lax
from jax.experimental import pallas as pl
from jax.experimental.pallas import tpu as pltpu
from jax.sharding import Mesh, PartitionSpec as P

HALVES, RING, LEVELS, ROWS, CELLS, SLAB = 2, 16, 8, 128, 256, 8
STOPS = 7
SEGMENTS = 8
STEPS = CELLS // SEGMENTS
SENT = 17
BACK = 10

VMEM = pl.BlockSpec(memory_space=pltpu.VMEM)


def lanes(shape):
    return lax.broadcasted_iota(jnp.int32, shape, len(shape) - 1)


def polar_start():
    lat = lax.axis_index("lat")
    last = lat == lax.axis_size("lat") - 1
    return (lat == 0) | last, pl.multiple_of(jnp.where(last, ROWS - SLAB, 0), SLAB)


def in_vmem(*arrays):
    return [pltpu.with_memory_space_constraint(x, pltpu.VMEM) for x in arrays]


def pack_kernel(
    tracer, courant, hops, area, sent, source_t, courant_t, entries, hops_out, area_out, source, factor, slab, sems
):
    rows = (
        pltpu.make_async_copy(hops, hops_out, sems.at[2, 0]),
        pltpu.make_async_copy(area, area_out, sems.at[2, 1]),
    )
    copies = [
        (
            pltpu.make_async_copy(tracer.at[l], source.at[l], sems.at[0, l]),
            pltpu.make_async_copy(courant.at[l], factor.at[l], sems.at[1, l]),
        )
        for l in range(LEVELS)
    ]
    for pair in (*copies, rows):
        for copy in pair:
            copy.start()
    _, start = polar_start()
    for l in range(LEVELS):
        for copy in copies[l]:
            copy.wait()
        source_t[pl.ds(l, CELLS, stride=LEVELS), :] = source[l].T
        courant_t[pl.ds(l, CELLS, stride=LEVELS), :] = factor[l].T
        for side in range(2):
            across = pl.ds(128 * side, 128)
            slab[side, pl.ds(SLAB * l, SLAB), :] = source[l, pl.ds(start, SLAB), across]
            slab[2 + side, pl.ds(SLAB * l, SLAB), :] = factor[l, pl.ds(start, SLAB), across]
    growth = [jnp.ones((LEVELS, ROWS), jnp.float32)] * SEGMENTS
    offset = [jnp.zeros((LEVELS, ROWS), jnp.float32)] * SEGMENTS
    for step in range(STEPS):
        for k in range(SEGMENTS):
            at = pl.ds(LEVELS * (STEPS * k + step), LEVELS)
            c = courant_t[at, :]
            f = 1.0 - 1.0 / (1.0 + c)
            offset[k] = f * (source_t[at, :] + offset[k])
            growth[k] = growth[k] * f
    g, o = growth[0], offset[0]
    for k in range(1, SEGMENTS):
        entries[2 * k] = g
        entries[2 * k + 1] = o
        g, o = g * growth[k], growth[k] * o + offset[k]
    low = lanes((LEVELS, ROWS)) < 64
    maps = (jnp.where(low, g, pltpu.roll(o, 64, 1)), jnp.where(low, pltpu.roll(g, 64, 1), o))
    for r in range(SLAB):
        for a in range(4):
            x = slab[a, pl.ds(r, LEVELS, stride=SLAB), :]
            sent[pl.ds(SENT * 2 * r + 4 * a, 4), :] = x[:4]
            sent[pl.ds(SENT * (2 * r + 1) + 4 * a, 4), :] = x[4:]
        for parity in range(2):
            sent[pl.ds(SENT * (2 * r + parity) + 16, 1), :] = maps[parity][r : r + 1]
    for copy in rows:
        copy.wait()


def pack(tracer, courant, hops, area):
    f32 = jnp.float32
    return pl.pallas_call(
        pack_kernel,
        out_shape=(
            pltpu.VMEM((RING * SENT, 128), f32),
            pltpu.VMEM((CELLS * LEVELS, ROWS), f32),
            pltpu.VMEM((CELLS * LEVELS, ROWS), f32),
            pltpu.VMEM((2 * SEGMENTS, LEVELS, ROWS), f32),
            pltpu.VMEM((1, ROWS), jnp.int32),
            pltpu.VMEM((1, ROWS), f32),
        ),
        in_specs=[pl.BlockSpec(memory_space=pl.ANY)] * 4,
        out_specs=(VMEM,) * 6,
        scratch_shapes=[
            pltpu.VMEM((LEVELS, ROWS, CELLS), f32),
            pltpu.VMEM((LEVELS, ROWS, CELLS), f32),
            pltpu.VMEM((4, LEVELS * SLAB, 128), f32),
            pltpu.SemaphoreType.DMA((3, LEVELS)),
        ],
        name="pack",
    )(tracer, courant, hops, area)


def solve_kernel(hops, area, own, far, far_maps, back, source, courant, source_t, courant_t):
    half = lax.axis_index("half")
    ring = lax.axis_index("ring")
    polar, start = polar_start()
    row, parity = ring // 2, ring % 2
    for d in range(HALVES * RING):
        ref, base = (own if d < RING else far), (d % RING) * SENT
        for side in range(2):
            to = pl.ds(side * 128, 128)
            source[pl.ds(4 * d, 4), to] = ref[pl.ds(base + 4 * side, 4), :]
            courant[pl.ds(4 * d, 4), to] = ref[pl.ds(base + 8 + 4 * side, 4), :]
    lane = lanes((1, 128))
    slab_row = lane == start + row
    hop = jnp.sum(jnp.where(slab_row, hops[...].astype(jnp.float32), 0.0), axis=1, keepdims=True).astype(jnp.int32)
    shifted = source[...].T
    for bit in range(STOPS.bit_length()):
        shifted = jnp.where((hop >> bit) % 2 == 1, pltpu.roll(shifted, 4 << bit, 1), shifted)
    source_t[...] = shifted
    courant_t[...] = courant[...].T
    parts = range(CELLS // 64)
    growth = [jnp.ones((8, ROWS), jnp.float32) for k in parts]
    offset = [jnp.zeros((8, ROWS), jnp.float32) for k in parts]
    for step in range(8):
        for k in parts:
            at = pl.ds(64 * k + step, 8, stride=8)
            c = courant_t[at, :]
            f = 1.0 - 1.0 / (1.0 + c)
            offset[k] = f * (source_t[at, :] + offset[k])
            growth[k] = growth[k] * f
    place = lax.broadcasted_iota(jnp.int32, (8, ROWS), 0)
    for stride in (1, 2, 4):
        inside = place >= stride
        for k in parts:
            offset[k] = jnp.where(inside, growth[k] * pltpu.roll(offset[k], stride, 0) + offset[k], offset[k])
            growth[k] = jnp.where(inside, growth[k] * pltpu.roll(growth[k], stride, 0), growth[k])
    g = jnp.ones((1, ROWS), jnp.float32)
    o = jnp.zeros((1, ROWS), jnp.float32)
    entry = []
    for k in parts:
        first = place == 0
        before_g = jnp.where(first, 1.0, pltpu.roll(growth[k], 1, 0))
        before_o = jnp.where(first, 0.0, pltpu.roll(offset[k], 1, 0))
        entry.append((before_g * g, before_g * o + before_o))
        g, o = g * growth[k][7:], growth[k][7:] * o + offset[k][7:]
    for stride in (4, 8, 16, 32, 64):
        o = g * pltpu.roll(o, stride, 1) + o
        g = g * pltpu.roll(g, stride, 1)
    inflow = pltpu.roll(o / (1.0 - g), 4, 1)
    flux = [entry[k][0] * inflow + entry[k][1] for k in parts]
    for step in range(8):
        for k in parts:
            at = pl.ds(64 * k + step, 8, stride=8)
            c = courant_t[at, :]
            u = (source_t[at, :] + flux[k]) * (1.0 / (1.0 + c))
            source_t[at, :] = u
            flux[k] = c * u
    source[...] = source_t[...].T
    at = pl.ds(16, RING, stride=SENT)
    x = jnp.concatenate([own[at, :], jnp.where(polar, far[at, :], far_maps[...])], 0)
    low = lanes(x.shape) < 64
    turned = pltpu.roll(x, 64, 1)
    rest_g = jnp.where(low, x, turned)
    rest_o = jnp.where(low, turned, x)
    for stride in (1, 2, 4, 8, 16):
        rest_o = rest_g * pltpu.roll(rest_o, stride, 0) + rest_o
        rest_g = rest_g * pltpu.roll(rest_g, stride, 0)
    rest = pltpu.roll(rest_o / (1.0 - rest_g), 1, 0)
    wrap = jnp.where(half == 0, rest[:1], rest[RING : RING + 1])
    areas = area[...]
    mine = lane // 64 == parity
    in_slab = polar & (lane >= start) & (lane < start + SLAB)
    weighted = jnp.where(mine & ~in_slab, areas, 0.0) * wrap
    weighted = jnp.sum(weighted, axis=1, keepdims=True)
    slab_area = jnp.sum(jnp.where(polar & slab_row, areas, 0.0), axis=1, keepdims=True)
    loops = pltpu.roll(inflow, (4 * parity + 128 - 64 * half) % 128, 1) * slab_area
    sums = jnp.where(lane == row, weighted, 0.0)
    sums = sums + jnp.where((lane >= 4 * parity) & (lane < 4 * parity + 4), loops, 0.0)
    total = jnp.sum(areas, axis=1, keepdims=True)
    sums = jnp.where(lane == 8, jnp.where(ring == 0, total, 0.0), sums)
    for d in range(RING):
        for side in range(2):
            back[pl.ds(BACK * d + 4 * side, 4), :] = source[pl.ds(4 * d, 4), pl.ds(side * 128, 128)]
        back[pl.ds(BACK * d + 8, 1), :] = rest[d : d + 1]
        back[pl.ds(BACK * d + 9, 1), :] = sums


def solve(hops, area, own, far, far_maps):
    f32 = jnp.float32
    return pl.pallas_call(
        solve_kernel,
        out_shape=pltpu.VMEM((RING * BACK, 128), f32),
        in_specs=[VMEM] * 5,
        out_specs=VMEM,
        scratch_shapes=[pltpu.VMEM((ROWS, CELLS), f32)] * 2 + [pltpu.VMEM((CELLS, ROWS), f32)] * 2,
        name="solve",
    )(*in_vmem(hops, area, own, far, far_maps))


def spread_kernel(got, sums):
    total = jnp.sum(got[pl.ds(9, RING, stride=BACK), :], axis=0, keepdims=True)
    for i in range(sums.shape[0]):
        sums[i] = total


def spread(got, lats):
    return pl.pallas_call(
        spread_kernel,
        out_shape=jax.ShapeDtypeStruct((lats, 1, 128), jnp.float32),
        in_specs=[VMEM],
        out_specs=VMEM,
        name="spread",
    )(*in_vmem(got))


def mean_kernel(sums, mean):
    total = sums[0]
    for i in range(1, sums.shape[0]):
        total = total + sums[i]
    area = jnp.sum(jnp.where(lanes((1, 128)) == 8, total, 0.0), axis=1, keepdims=True)
    mean[...] = (total / area)[0, :LEVELS]


def mean(sums):
    return pl.pallas_call(
        mean_kernel,
        out_shape=jax.ShapeDtypeStruct((LEVELS,), jnp.float32),
        in_specs=[VMEM],
        out_specs=VMEM,
        name="mean",
    )(*in_vmem(sums))


def finish_kernel(source_t, courant_t, entries, got, updated, updated_t, level, sems):
    low = lanes((LEVELS, ROWS)) < 64
    even = got[pl.ds(8, LEVELS, stride=2 * BACK), :]
    odd = got[pl.ds(8 + BACK, LEVELS, stride=2 * BACK), :]
    inflow = jnp.where(low, even, odd)
    flux = [inflow] + [entries[2 * k] * inflow + entries[2 * k + 1] for k in range(1, SEGMENTS)]
    for step in range(STEPS):
        for k in range(SEGMENTS):
            at = pl.ds(LEVELS * (STEPS * k + step), LEVELS)
            c = courant_t[at, :]
            u = (source_t[at, :] + flux[k]) * (1.0 / (1.0 + c))
            updated_t[at, :] = u
            flux[k] = c * u
    polar, start = polar_start()
    rows = pl.ds(start, SLAB)
    copies = []
    for l in range(LEVELS):
        level[l] = updated_t[pl.ds(l, CELLS, stride=LEVELS), :].T
        for side in range(2):
            to = pl.ds(side * 128, 128)
            at = (l // 4) * BACK + 4 * side + l % 4
            solved = got[pl.ds(at, SLAB, stride=2 * BACK), :]
            level[l, rows, to] = jnp.where(polar, solved, level[l, rows, to])
        copies.append(pltpu.make_async_copy(level.at[l], updated.at[l], sems.at[l]))
        copies[l].start()
    for copy in copies:
        copy.wait()


def finish(source_t, courant_t, entries, got):
    f32 = jnp.float32
    return pl.pallas_call(
        finish_kernel,
        out_shape=jax.ShapeDtypeStruct((LEVELS, ROWS, CELLS), f32),
        in_specs=[VMEM] * 4,
        out_specs=pl.BlockSpec(memory_space=pl.ANY),
        scratch_shapes=[
            pltpu.VMEM((CELLS * LEVELS, ROWS), f32),
            pltpu.VMEM((LEVELS, ROWS, CELLS), f32),
            pltpu.SemaphoreType.DMA((LEVELS,)),
        ],
        name="finish",
    )(*in_vmem(source_t, courant_t, entries, got))


def exchange(rows):
    blocks = rows.reshape(RING, -1, 1, 128)
    return lax.all_to_all(blocks, "ring", 0, 0, tiled=True).reshape(rows.shape)


def body(tracer, courant, hop_counts, row_area):
    lats = lax.axis_size("lat")

    def across(polar):
        half = RING * lats
        pairs = []
        for i in range(HALVES * half):
            moved = (i % lats in (0, lats - 1)) == polar
            pairs.append((i, (i + half) % (HALVES * half) if moved else i))
        return pairs

    hops, area = hop_counts.reshape(1, ROWS), row_area.reshape(1, ROWS)
    sent, source_t, courant_t, entries, hops, area = pack(tracer, courant, hops, area)
    got = exchange(sent)
    every = ("half", "ring", "lat")
    far = lax.ppermute(got, every, across(True))
    far_maps = lax.ppermute(lax.slice(got, (16, 0), (RING * SENT, 128), (SENT, 1)), every, across(False))
    back = solve(hops, area, got, far, far_maps)
    back = exchange(back)
    sums = lax.all_to_all(spread(back, lats), "lat", 0, 0, tiled=True)
    return finish(source_t, courant_t, entries, back), mean(sums)


def solution(mesh):
    split = Mesh(mesh.devices.reshape(HALVES, RING, -1), ("half", "ring", "lat"))
    field = P(None, "lat", ("half", "ring"))
    return jax.shard_map(
        body,
        mesh=split,
        in_specs=(field, field, P("lat"), P("lat")),
        out_specs=(field, P()),
        check_vma=False,
    )
```

```python
import jax
import jax.numpy as jnp
from jax import lax
from jax.experimental import pallas as pl
from jax.experimental.pallas import tpu as pltpu
from jax.sharding import Mesh, PartitionSpec as P

HALVES, RING, LEVELS, ROWS, CELLS, SLAB = 2, 16, 8, 128, 256, 8
STOPS = 7
SEGMENTS = 8
STEPS = CELLS // SEGMENTS
SENT = 17
BACK = 9

VMEM = pl.BlockSpec(memory_space=pltpu.VMEM)


def lanes(shape):
    return lax.broadcasted_iota(jnp.int32, shape, len(shape) - 1)


def polar_start():
    lat = lax.axis_index("lat")
    last = lat == lax.axis_size("lat") - 1
    return (lat == 0) | last, pl.multiple_of(jnp.where(last, ROWS - SLAB, 0), SLAB)


def in_vmem(*arrays):
    return [pltpu.with_memory_space_constraint(x, pltpu.VMEM) for x in arrays]


def pack_kernel(
    tracer, courant, hops, area, sent, source_t, courant_t, entries, hops_out, area_out, source, factor, sems
):
    rows = (
        pltpu.make_async_copy(hops, hops_out, sems.at[2, 0]),
        pltpu.make_async_copy(area, area_out, sems.at[2, 1]),
    )
    copies = [
        (
            pltpu.make_async_copy(tracer.at[l], source.at[l], sems.at[0, l]),
            pltpu.make_async_copy(courant.at[l], factor.at[l], sems.at[1, l]),
        )
        for l in range(LEVELS)
    ]
    for pair in (*copies, rows):
        for copy in pair:
            copy.start()
    _, start = polar_start()
    for l in range(LEVELS):
        for copy in copies[l]:
            copy.wait()
        source_t[pl.ds(l, CELLS, stride=LEVELS), :] = source[l].T
        courant_t[pl.ds(l, CELLS, stride=LEVELS), :] = factor[l].T
        for side in range(2):
            across = pl.ds(128 * side, 128)
            for a, field in enumerate((source, factor)):
                to = pl.ds(SENT * (l // 4) + 8 * a + 4 * side + l % 4, SLAB, stride=2 * SENT)
                sent[to, :] = field[l, pl.ds(start, SLAB), across]
    growth = [jnp.ones((LEVELS, ROWS), jnp.float32)] * SEGMENTS
    offset = [jnp.zeros((LEVELS, ROWS), jnp.float32)] * SEGMENTS
    for step in range(STEPS):
        for k in range(SEGMENTS):
            at = pl.ds(LEVELS * (STEPS * k + step), LEVELS)
            c = courant_t[at, :]
            f = 1.0 - 1.0 / (1.0 + c)
            offset[k] = f * (source_t[at, :] + offset[k])
            growth[k] = growth[k] * f
    g, o = growth[0], offset[0]
    for k in range(1, SEGMENTS):
        entries[2 * k] = g
        entries[2 * k + 1] = o
        g, o = g * growth[k], growth[k] * o + offset[k]
    low = lanes((LEVELS, ROWS)) < 64
    maps = (jnp.where(low, g, pltpu.roll(o, 64, 1)), jnp.where(low, pltpu.roll(g, 64, 1), o))
    for l in range(LEVELS):
        for parity in range(2):
            sent[pl.ds(SENT * (2 * l + parity) + 16, 1), :] = maps[parity][l : l + 1]
    for copy in rows:
        copy.wait()


def pack(tracer, courant, hops, area):
    f32 = jnp.float32
    return pl.pallas_call(
        pack_kernel,
        out_shape=(
            pltpu.VMEM((RING * SENT, 128), f32),
            pltpu.VMEM((CELLS * LEVELS, ROWS), f32),
            pltpu.VMEM((CELLS * LEVELS, ROWS), f32),
            pltpu.VMEM((2 * SEGMENTS, LEVELS, ROWS), f32),
            pltpu.VMEM((1, ROWS), jnp.int32),
            pltpu.VMEM((1, ROWS), f32),
        ),
        in_specs=[pl.BlockSpec(memory_space=pl.ANY)] * 4,
        out_specs=(VMEM,) * 6,
        scratch_shapes=[
            pltpu.VMEM((LEVELS, ROWS, CELLS), f32),
            pltpu.VMEM((LEVELS, ROWS, CELLS), f32),
            pltpu.SemaphoreType.DMA((3, LEVELS)),
        ],
        name="pack",
    )(tracer, courant, hops, area)


def solve_kernel(hops, area, own, far, far_maps, back, source, courant, source_t, courant_t):
    half = lax.axis_index("half")
    ring = lax.axis_index("ring")
    polar, start = polar_start()
    row, parity = ring // 2, ring % 2
    for d in range(HALVES * RING):
        ref, base = (own if d < RING else far), (d % RING) * SENT
        for side in range(2):
            to = pl.ds(side * 128, 128)
            source[pl.ds(4 * d, 4), to] = ref[pl.ds(base + 4 * side, 4), :]
            courant[pl.ds(4 * d, 4), to] = ref[pl.ds(base + 8 + 4 * side, 4), :]
    lane = lanes((1, 128))
    slab_row = lane == start + row
    hop = jnp.sum(jnp.where(slab_row, hops[...].astype(jnp.float32), 0.0), axis=1, keepdims=True).astype(jnp.int32)
    shifted = source[...].T
    for bit in range(STOPS.bit_length()):
        shifted = jnp.where((hop >> bit) % 2 == 1, pltpu.roll(shifted, 4 << bit, 1), shifted)
    source_t[...] = shifted
    courant_t[...] = courant[...].T
    parts = range(CELLS // 64)
    growth = [jnp.ones((8, ROWS), jnp.float32) for k in parts]
    offset = [jnp.zeros((8, ROWS), jnp.float32) for k in parts]
    for step in range(8):
        for k in parts:
            at = pl.ds(64 * k + step, 8, stride=8)
            c = courant_t[at, :]
            f = 1.0 - 1.0 / (1.0 + c)
            offset[k] = f * (source_t[at, :] + offset[k])
            growth[k] = growth[k] * f
    place = lax.broadcasted_iota(jnp.int32, (8, ROWS), 0)
    for stride in (1, 2, 4):
        inside = place >= stride
        for k in parts:
            offset[k] = jnp.where(inside, growth[k] * pltpu.roll(offset[k], stride, 0) + offset[k], offset[k])
            growth[k] = jnp.where(inside, growth[k] * pltpu.roll(growth[k], stride, 0), growth[k])
    g = jnp.ones((1, ROWS), jnp.float32)
    o = jnp.zeros((1, ROWS), jnp.float32)
    entry = []
    for k in parts:
        first = place == 0
        before_g = jnp.where(first, 1.0, pltpu.roll(growth[k], 1, 0))
        before_o = jnp.where(first, 0.0, pltpu.roll(offset[k], 1, 0))
        entry.append((before_g * g, before_g * o + before_o))
        g, o = g * growth[k][7:], growth[k][7:] * o + offset[k][7:]
    for stride in (4, 8, 16, 32, 64):
        o = g * pltpu.roll(o, stride, 1) + o
        g = g * pltpu.roll(g, stride, 1)
    inflow = pltpu.roll(o / (1.0 - g), 4, 1)
    flux = [entry[k][0] * inflow + entry[k][1] for k in parts]
    for step in range(8):
        for k in parts:
            at = pl.ds(64 * k + step, 8, stride=8)
            c = courant_t[at, :]
            u = (source_t[at, :] + flux[k]) * (1.0 / (1.0 + c))
            source_t[at, :] = u
            flux[k] = c * u
    source[...] = source_t[...].T
    at = pl.ds(16, RING, stride=SENT)
    x = jnp.concatenate([own[at, :], jnp.where(polar, far[at, :], far_maps[...])], 0)
    low = lanes(x.shape) < 64
    turned = pltpu.roll(x, 64, 1)
    rest_g = jnp.where(low, x, turned)
    rest_o = jnp.where(low, turned, x)
    for stride in (1, 2, 4, 8, 16):
        rest_o = rest_g * pltpu.roll(rest_o, stride, 0) + rest_o
        rest_g = rest_g * pltpu.roll(rest_g, stride, 0)
    rest = pltpu.roll(rest_o / (1.0 - rest_g), 1, 0)
    wrap = jnp.where(half == 0, rest[:1], rest[RING : RING + 1])
    areas = area[...]
    mine = lane // 64 == parity
    in_slab = polar & (lane >= start) & (lane < start + SLAB)
    weighted = jnp.where(mine & ~in_slab, areas, 0.0) * wrap
    weighted = jnp.sum(weighted, axis=1, keepdims=True)
    slab_area = jnp.sum(jnp.where(polar & slab_row, areas, 0.0), axis=1, keepdims=True)
    loops = pltpu.roll(inflow, (4 * parity + 128 - 64 * half) % 128, 1) * slab_area
    sums = jnp.where(lane == row, weighted, 0.0)
    sums = sums + jnp.where((lane >= 4 * parity) & (lane < 4 * parity + 4), loops, 0.0)
    total = jnp.sum(areas, axis=1, keepdims=True)
    sums = jnp.where(lane == 8, jnp.where(ring == 0, total, 0.0), sums)
    sums = pltpu.roll(sums, 64, 1)
    for d in range(RING):
        for side in range(2):
            back[pl.ds(BACK * d + 4 * side, 4), :] = source[pl.ds(4 * d, 4), pl.ds(side * 128, 128)]
        back[pl.ds(BACK * d + 8, 1), :] = jnp.where(lane < 64, rest[d : d + 1], sums)


def solve(hops, area, own, far, far_maps):
    f32 = jnp.float32
    return pl.pallas_call(
        solve_kernel,
        out_shape=pltpu.VMEM((RING * BACK, 128), f32),
        in_specs=[VMEM] * 5,
        out_specs=VMEM,
        scratch_shapes=[pltpu.VMEM((ROWS, CELLS), f32)] * 2 + [pltpu.VMEM((CELLS, ROWS), f32)] * 2,
        name="solve",
    )(*in_vmem(hops, area, own, far, far_maps))


def spread_kernel(got, sums):
    total = pltpu.roll(jnp.sum(got[pl.ds(8, RING, stride=BACK), :], axis=0, keepdims=True), 64, 1)
    for i in range(sums.shape[0]):
        sums[i] = total


def spread(got, lats):
    return pl.pallas_call(
        spread_kernel,
        out_shape=jax.ShapeDtypeStruct((lats, 1, 128), jnp.float32),
        in_specs=[VMEM],
        out_specs=VMEM,
        name="spread",
    )(*in_vmem(got))


def mean_kernel(sums, mean):
    total = sums[0]
    for i in range(1, sums.shape[0]):
        total = total + sums[i]
    area = jnp.sum(jnp.where(lanes((1, 128)) == 8, total, 0.0), axis=1, keepdims=True)
    mean[...] = (total / area)[0, :LEVELS]


def mean(sums):
    return pl.pallas_call(
        mean_kernel,
        out_shape=jax.ShapeDtypeStruct((LEVELS,), jnp.float32),
        in_specs=[VMEM],
        out_specs=VMEM,
        name="mean",
    )(*in_vmem(sums))


def finish_kernel(source_t, courant_t, entries, got, updated, updated_t, level, sems):
    low = lanes((LEVELS, ROWS)) < 64
    even = got[pl.ds(8, LEVELS, stride=2 * BACK), :]
    odd = got[pl.ds(8 + BACK, LEVELS, stride=2 * BACK), :]
    inflow = jnp.where(low, even, pltpu.roll(odd, 64, 1))
    flux = [inflow] + [entries[2 * k] * inflow + entries[2 * k + 1] for k in range(1, SEGMENTS)]
    for step in range(STEPS):
        for k in range(SEGMENTS):
            at = pl.ds(LEVELS * (STEPS * k + step), LEVELS)
            c = courant_t[at, :]
            u = (source_t[at, :] + flux[k]) * (1.0 / (1.0 + c))
            updated_t[at, :] = u
            flux[k] = c * u
    polar, start = polar_start()
    rows = pl.ds(start, SLAB)
    copies = []
    for l in range(LEVELS):
        level[l] = updated_t[pl.ds(l, CELLS, stride=LEVELS), :].T
        for side in range(2):
            to = pl.ds(side * 128, 128)
            at = (l // 4) * BACK + 4 * side + l % 4
            solved = got[pl.ds(at, SLAB, stride=2 * BACK), :]
            level[l, rows, to] = jnp.where(polar, solved, level[l, rows, to])
        copies.append(pltpu.make_async_copy(level.at[l], updated.at[l], sems.at[l]))
        copies[l].start()
    for copy in copies:
        copy.wait()


def finish(source_t, courant_t, entries, got):
    f32 = jnp.float32
    return pl.pallas_call(
        finish_kernel,
        out_shape=jax.ShapeDtypeStruct((LEVELS, ROWS, CELLS), f32),
        in_specs=[VMEM] * 4,
        out_specs=pl.BlockSpec(memory_space=pl.ANY),
        scratch_shapes=[
            pltpu.VMEM((CELLS * LEVELS, ROWS), f32),
            pltpu.VMEM((LEVELS, ROWS, CELLS), f32),
            pltpu.SemaphoreType.DMA((LEVELS,)),
        ],
        name="finish",
    )(*in_vmem(source_t, courant_t, entries, got))


def exchange(rows):
    blocks = rows.reshape(RING, -1, 1, 128)
    return lax.all_to_all(blocks, "ring", 0, 0, tiled=True).reshape(rows.shape)


def body(tracer, courant, hop_counts, row_area):
    lats = lax.axis_size("lat")

    def across(polar):
        half = RING * lats
        pairs = []
        for i in range(HALVES * half):
            moved = (i % lats in (0, lats - 1)) == polar
            pairs.append((i, (i + half) % (HALVES * half) if moved else i))
        return pairs

    hops, area = hop_counts.reshape(1, ROWS), row_area.reshape(1, ROWS)
    sent, source_t, courant_t, entries, hops, area = pack(tracer, courant, hops, area)
    got = exchange(sent)
    every = ("half", "ring", "lat")
    far = lax.ppermute(got, every, across(True))
    far_maps = lax.ppermute(lax.slice(got, (16, 0), (RING * SENT, 128), (SENT, 1)), every, across(False))
    back = solve(hops, area, got, far, far_maps)
    back = exchange(back)
    sums = lax.all_to_all(spread(back, lats), "lat", 0, 0, tiled=True)
    return finish(source_t, courant_t, entries, back), mean(sums)


def solution(mesh):
    split = Mesh(mesh.devices.reshape(HALVES, RING, -1), ("half", "ring", "lat"))
    field = P(None, "lat", ("half", "ring"))
    return jax.shard_map(
        body,
        mesh=split,
        in_specs=(field, field, P("lat"), P("lat")),
        out_specs=(field, P()),
        check_vma=False,
    )
```

```python
import jax
import jax.numpy as jnp
from jax import lax
from jax.experimental import pallas as pl
from jax.experimental.pallas import tpu as pltpu
from jax.sharding import Mesh, PartitionSpec as P

HALVES, RING, LEVELS, ROWS, CELLS, SLAB = 2, 16, 8, 128, 256, 8
STOPS = 7
SEGMENTS = 8
STEPS = CELLS // SEGMENTS
SENT = 17
BACK = 9

VMEM = pl.BlockSpec(memory_space=pltpu.VMEM)


def lanes(shape):
    return lax.broadcasted_iota(jnp.int32, shape, len(shape) - 1)


def polar_start():
    lat = lax.axis_index("lat")
    last = lat == lax.axis_size("lat") - 1
    return (lat == 0) | last, pl.multiple_of(jnp.where(last, ROWS - SLAB, 0), SLAB)


def in_vmem(*arrays):
    return [pltpu.with_memory_space_constraint(x, pltpu.VMEM) for x in arrays]


def pack_kernel(
    tracer, courant, hops, area, sent, source_t, courant_t, entries, hops_out, area_out, source, factor, sems
):
    rows = (
        pltpu.make_async_copy(hops, hops_out, sems.at[2, 0]),
        pltpu.make_async_copy(area, area_out, sems.at[2, 1]),
    )
    copies = [
        (
            pltpu.make_async_copy(tracer.at[l], source.at[l], sems.at[0, l]),
            pltpu.make_async_copy(courant.at[l], factor.at[l], sems.at[1, l]),
        )
        for l in range(LEVELS)
    ]
    for pair in (*copies, rows):
        for copy in pair:
            copy.start()
    _, start = polar_start()
    for l in range(LEVELS):
        if l % 2 == 0:
            for copy in (*copies[l], *copies[l + 1]):
                copy.wait()
        source_t[pl.ds(l, CELLS, stride=LEVELS), :] = source[l].T
        courant_t[pl.ds(l, CELLS, stride=LEVELS), :] = factor[l].T
        for side in range(2):
            across = pl.ds(128 * side, 128)
            for a, field in enumerate((source, factor)):
                to = pl.ds(SENT * (l // 4) + 8 * a + 4 * side + l % 4, SLAB, stride=2 * SENT)
                sent[to, :] = field[l, pl.ds(start, SLAB), across]
    growth = [jnp.ones((LEVELS, ROWS), jnp.float32)] * SEGMENTS
    offset = [jnp.zeros((LEVELS, ROWS), jnp.float32)] * SEGMENTS
    for step in range(STEPS):
        for k in range(SEGMENTS):
            at = pl.ds(LEVELS * (STEPS * k + step), LEVELS)
            c = courant_t[at, :]
            f = 1.0 - 1.0 / (1.0 + c)
            offset[k] = f * (source_t[at, :] + offset[k])
            growth[k] = growth[k] * f
    g, o = growth[0], offset[0]
    for k in range(1, SEGMENTS):
        entries[2 * k] = g
        entries[2 * k + 1] = o
        g, o = g * growth[k], growth[k] * o + offset[k]
    low = lanes((LEVELS, ROWS)) < 64
    maps = (jnp.where(low, g, pltpu.roll(o, 64, 1)), jnp.where(low, pltpu.roll(g, 64, 1), o))
    for l in range(LEVELS):
        for parity in range(2):
            sent[pl.ds(SENT * (2 * l + parity) + 16, 1), :] = maps[parity][l : l + 1]
    for copy in rows:
        copy.wait()


def pack(tracer, courant, hops, area):
    f32 = jnp.float32
    return pl.pallas_call(
        pack_kernel,
        out_shape=(
            pltpu.VMEM((RING * SENT, 128), f32),
            pltpu.VMEM((CELLS * LEVELS, ROWS), f32),
            pltpu.VMEM((CELLS * LEVELS, ROWS), f32),
            pltpu.VMEM((2 * SEGMENTS, LEVELS, ROWS), f32),
            pltpu.VMEM((1, ROWS), jnp.int32),
            pltpu.VMEM((1, ROWS), f32),
        ),
        in_specs=[pl.BlockSpec(memory_space=pl.ANY)] * 4,
        out_specs=(VMEM,) * 6,
        scratch_shapes=[
            pltpu.VMEM((LEVELS, ROWS, CELLS), f32),
            pltpu.VMEM((LEVELS, ROWS, CELLS), f32),
            pltpu.SemaphoreType.DMA((3, LEVELS)),
        ],
        name="pack",
    )(tracer, courant, hops, area)


def solve_kernel(hops, area, own, far, far_maps, back, source, courant, source_t, courant_t):
    half = lax.axis_index("half")
    ring = lax.axis_index("ring")
    polar, start = polar_start()
    row, parity = ring // 2, ring % 2
    for d in range(HALVES * RING):
        ref, base = (own if d < RING else far), (d % RING) * SENT
        for side in range(2):
            to = pl.ds(side * 128, 128)
            source[pl.ds(4 * d, 4), to] = ref[pl.ds(base + 4 * side, 4), :]
            courant[pl.ds(4 * d, 4), to] = ref[pl.ds(base + 8 + 4 * side, 4), :]
    lane = lanes((1, 128))
    slab_row = lane == start + row
    hop = jnp.sum(jnp.where(slab_row, hops[...].astype(jnp.float32), 0.0), axis=1, keepdims=True).astype(jnp.int32)
    shifted = source[...].T
    for bit in range(STOPS.bit_length()):
        shifted = jnp.where((hop >> bit) % 2 == 1, pltpu.roll(shifted, 4 << bit, 1), shifted)
    source_t[...] = shifted
    courant_t[...] = courant[...].T
    parts = range(CELLS // 64)
    growth = [jnp.ones((8, ROWS), jnp.float32) for k in parts]
    offset = [jnp.zeros((8, ROWS), jnp.float32) for k in parts]
    for step in range(8):
        for k in parts:
            at = pl.ds(64 * k + step, 8, stride=8)
            c = courant_t[at, :]
            f = 1.0 - 1.0 / (1.0 + c)
            offset[k] = f * (source_t[at, :] + offset[k])
            growth[k] = growth[k] * f
    place = lax.broadcasted_iota(jnp.int32, (8, ROWS), 0)
    for stride in (1, 2, 4):
        inside = place >= stride
        for k in parts:
            offset[k] = jnp.where(inside, growth[k] * pltpu.roll(offset[k], stride, 0) + offset[k], offset[k])
            growth[k] = jnp.where(inside, growth[k] * pltpu.roll(growth[k], stride, 0), growth[k])
    g = jnp.ones((1, ROWS), jnp.float32)
    o = jnp.zeros((1, ROWS), jnp.float32)
    entry = []
    for k in parts:
        first = place == 0
        before_g = jnp.where(first, 1.0, pltpu.roll(growth[k], 1, 0))
        before_o = jnp.where(first, 0.0, pltpu.roll(offset[k], 1, 0))
        entry.append((before_g * g, before_g * o + before_o))
        g, o = g * growth[k][7:], growth[k][7:] * o + offset[k][7:]
    for stride in (4, 8, 16, 32, 64):
        o = g * pltpu.roll(o, stride, 1) + o
        g = g * pltpu.roll(g, stride, 1)
    inflow = pltpu.roll(o / (1.0 - g), 4, 1)
    flux = [entry[k][0] * inflow + entry[k][1] for k in parts]
    for step in range(8):
        for k in parts:
            at = pl.ds(64 * k + step, 8, stride=8)
            c = courant_t[at, :]
            u = (source_t[at, :] + flux[k]) * (1.0 / (1.0 + c))
            source_t[at, :] = u
            flux[k] = c * u
    source[...] = source_t[...].T
    at = pl.ds(16, RING, stride=SENT)
    x = jnp.concatenate([own[at, :], jnp.where(polar, far[at, :], far_maps[...])], 0)
    low = lanes(x.shape) < 64
    turned = pltpu.roll(x, 64, 1)
    rest_g = jnp.where(low, x, turned)
    rest_o = jnp.where(low, turned, x)
    for stride in (1, 2, 4, 8, 16):
        rest_o = rest_g * pltpu.roll(rest_o, stride, 0) + rest_o
        rest_g = rest_g * pltpu.roll(rest_g, stride, 0)
    rest = pltpu.roll(rest_o / (1.0 - rest_g), 1, 0)
    wrap = jnp.where(half == 0, rest[:1], rest[RING : RING + 1])
    areas = area[...]
    mine = lane // 64 == parity
    in_slab = polar & (lane >= start) & (lane < start + SLAB)
    weighted = jnp.where(mine & ~in_slab, areas, 0.0) * wrap
    weighted = jnp.sum(weighted, axis=1, keepdims=True)
    slab_area = jnp.sum(jnp.where(polar & slab_row, areas, 0.0), axis=1, keepdims=True)
    loops = pltpu.roll(inflow, (4 * parity + 128 - 64 * half) % 128, 1) * slab_area
    sums = jnp.where(lane == row, weighted, 0.0)
    sums = sums + jnp.where((lane >= 4 * parity) & (lane < 4 * parity + 4), loops, 0.0)
    total = jnp.sum(areas, axis=1, keepdims=True)
    sums = jnp.where(lane == 8, jnp.where(ring == 0, total, 0.0), sums)
    sums = pltpu.roll(sums, 64, 1)
    for d in range(RING):
        for side in range(2):
            back[pl.ds(BACK * d + 4 * side, 4), :] = source[pl.ds(4 * d, 4), pl.ds(side * 128, 128)]
        back[pl.ds(BACK * d + 8, 1), :] = jnp.where(lane < 64, rest[d : d + 1], sums)


def solve(hops, area, own, far, far_maps):
    f32 = jnp.float32
    return pl.pallas_call(
        solve_kernel,
        out_shape=pltpu.VMEM((RING * BACK, 128), f32),
        in_specs=[VMEM] * 5,
        out_specs=VMEM,
        scratch_shapes=[pltpu.VMEM((ROWS, CELLS), f32)] * 2 + [pltpu.VMEM((CELLS, ROWS), f32)] * 2,
        name="solve",
    )(*in_vmem(hops, area, own, far, far_maps))


def spread_kernel(got, sums):
    total = pltpu.roll(jnp.sum(got[pl.ds(8, RING, stride=BACK), :], axis=0, keepdims=True), 64, 1)
    for i in range(sums.shape[0]):
        sums[i] = total


def spread(got, lats):
    return pl.pallas_call(
        spread_kernel,
        out_shape=jax.ShapeDtypeStruct((lats, 1, 128), jnp.float32),
        in_specs=[VMEM],
        out_specs=VMEM,
        name="spread",
    )(*in_vmem(got))


def mean_kernel(sums, mean):
    total = sums[0]
    for i in range(1, sums.shape[0]):
        total = total + sums[i]
    area = jnp.sum(jnp.where(lanes((1, 128)) == 8, total, 0.0), axis=1, keepdims=True)
    mean[...] = (total / area)[0, :LEVELS]


def mean(sums):
    return pl.pallas_call(
        mean_kernel,
        out_shape=jax.ShapeDtypeStruct((LEVELS,), jnp.float32),
        in_specs=[VMEM],
        out_specs=VMEM,
        name="mean",
    )(*in_vmem(sums))


def finish_kernel(source_t, courant_t, entries, got, updated, updated_t, level, sems):
    low = lanes((LEVELS, ROWS)) < 64
    even = got[pl.ds(8, LEVELS, stride=2 * BACK), :]
    odd = got[pl.ds(8 + BACK, LEVELS, stride=2 * BACK), :]
    inflow = jnp.where(low, even, pltpu.roll(odd, 64, 1))
    flux = [inflow] + [entries[2 * k] * inflow + entries[2 * k + 1] for k in range(1, SEGMENTS)]
    for step in range(STEPS):
        for k in range(SEGMENTS):
            at = pl.ds(LEVELS * (STEPS * k + step), LEVELS)
            c = courant_t[at, :]
            u = (source_t[at, :] + flux[k]) * (1.0 / (1.0 + c))
            updated_t[at, :] = u
            flux[k] = c * u
    polar, start = polar_start()
    rows = pl.ds(start, SLAB)
    copies = []
    for l in range(LEVELS):
        level[l] = updated_t[pl.ds(l, CELLS, stride=LEVELS), :].T
        for side in range(2):
            to = pl.ds(side * 128, 128)
            at = (l // 4) * BACK + 4 * side + l % 4
            solved = got[pl.ds(at, SLAB, stride=2 * BACK), :]
            level[l, rows, to] = jnp.where(polar, solved, level[l, rows, to])
        copies.append(pltpu.make_async_copy(level.at[l], updated.at[l], sems.at[l]))
        copies[l].start()
    for copy in copies:
        copy.wait()


def finish(source_t, courant_t, entries, got):
    f32 = jnp.float32
    return pl.pallas_call(
        finish_kernel,
        out_shape=jax.ShapeDtypeStruct((LEVELS, ROWS, CELLS), f32),
        in_specs=[VMEM] * 4,
        out_specs=pl.BlockSpec(memory_space=pl.ANY),
        scratch_shapes=[
            pltpu.VMEM((CELLS * LEVELS, ROWS), f32),
            pltpu.VMEM((LEVELS, ROWS, CELLS), f32),
            pltpu.SemaphoreType.DMA((LEVELS,)),
        ],
        name="finish",
    )(*in_vmem(source_t, courant_t, entries, got))


def exchange(rows):
    blocks = rows.reshape(RING, -1, 1, 128)
    return lax.all_to_all(blocks, "ring", 0, 0, tiled=True).reshape(rows.shape)


def body(tracer, courant, hop_counts, row_area):
    lats = lax.axis_size("lat")

    def across(polar):
        half = RING * lats
        pairs = []
        for i in range(HALVES * half):
            moved = (i % lats in (0, lats - 1)) == polar
            pairs.append((i, (i + half) % (HALVES * half) if moved else i))
        return pairs

    hops, area = hop_counts.reshape(1, ROWS), row_area.reshape(1, ROWS)
    sent, source_t, courant_t, entries, hops, area = pack(tracer, courant, hops, area)
    got = exchange(sent)
    every = ("half", "ring", "lat")
    far = lax.ppermute(got, every, across(True))
    far_maps = lax.ppermute(lax.slice(got, (16, 0), (RING * SENT, 128), (SENT, 1)), every, across(False))
    back = solve(hops, area, got, far, far_maps)
    back = exchange(back)
    sums = lax.all_to_all(spread(back, lats), "lat", 0, 0, tiled=True)
    return finish(source_t, courant_t, entries, back), mean(sums)


def solution(mesh):
    split = Mesh(mesh.devices.reshape(HALVES, RING, -1), ("half", "ring", "lat"))
    field = P(None, "lat", ("half", "ring"))
    return jax.shard_map(
        body,
        mesh=split,
        in_specs=(field, field, P("lat"), P("lat")),
        out_specs=(field, P()),
        check_vma=False,
    )
```
